128 devices in a mesh: section: 8 (over y, core), fsdp: 16 (over x, z).
Axes of the slice: x: 4, y: 4, z: 4, core: 2. Of those that a mesh axis runs over, the one named last changes fastest.
Arguments:
- layer_input: bfloat16 [8, 8192, 2048], P('section', 'fsdp'), may hold values from -6 to 6
- resid_grad: bfloat16 [8, 8192, 2048], P('section', 'fsdp'), may hold values from -6 to 6
- qkv_grad: bfloat16 [8, 8192, 3072], P('section', 'fsdp'), may hold values from -6 to 6
- prev_input: bfloat16 [8, 8192, 2048], P('section', 'fsdp'), may hold values from -6 to 6
- prev_qkv_grad: bfloat16 [8, 8192, 3072], P('section', 'fsdp'), may hold values from -0.059814453 to 0.059814453
- qkv_weight: bfloat16 [8, 2048, 3072], P('section', 'fsdp'), may hold values from -0.125 to 0.125
- norm_gain: float32 [8, 2048], P('section'), may hold values from 0.1 to 1.9
Outputs:
- upstream_grad: bfloat16 [8, 8192, 2048], P('section', 'fsdp')
- weight_grad: float32 [8, 2048, 3072], P('section', 'fsdp')
- gain_grad: float32 [8, 2048], P('section')
The draws below stay inside these ranges and needn't reach their ends.
All inputs are finite; a program needn't handle non-finite values.
Results may differ from the reference program's by a relative error of at most 0.018.
Values may be sent and summed in bfloat16 or wider, within the bound.
A program may use at most 128 MiB of HBM per device.

```python
import jax
import jax.numpy as jnp
from jax import lax

D = 2048
TOK_DEV = 512
QKV = 3072
TOKENS = 8192
N_SECTION = 8
N_FSDP = 16


def spiked(values, key, source, target, blocks, factor):
    owner, partner = [(jnp.arange(values.shape[position]) // (values.shape[position] // blocks)).reshape([-1 if axis == position else 1 for axis in range(values.ndim)]) for position in (source, target)]
    chosen = jax.random.permutation(key, blocks)[partner]
    strong = (owner == chosen) | (owner == (partner + blocks // 2) % blocks)
    return jnp.where(strong, factor * values, values)


def level_of(rng, extent, shards, least, largest):
    def one(axis_at, shards_of):
        steps = jax.random.uniform(jax.random.fold_in(jax.random.fold_in(rng, 6), axis_at), (shards_of,), jnp.float32, least / len(shards), largest / len(shards))
        return jnp.repeat(jnp.exp(steps), extent[axis_at] // shards_of).reshape((-1,) + (1,) * (len(extent) - axis_at - 1))

    factor_of = one(*shards[0])
    for cut in shards[1:]:
        factor_of = factor_of * one(*cut)
    return factor_of


def noise(own_key, shape, deviation, most, shards=(), held_as=jnp.bfloat16):
    array = jax.random.normal(own_key, shape, jnp.float32) * deviation
    if len(shards) > 0:
        array = level_of(own_key, shape, shards, -0.22, 0.18) * array
    return jnp.clip(array, min=-most, max=most).astype(held_as)


def bell_draw_with(stream_key, dims, scale, most, cuts, heavy, dtype=jnp.bfloat16):
    drawn = scale * jax.random.normal(stream_key, dims, jnp.float32)
    if cuts:
        drawn = drawn * level_of(stream_key, dims, cuts, -0.22, 0.18)
    return jnp.clip(spiked(drawn, jax.random.fold_in(stream_key, 3), *heavy), -most, most).astype(dtype)


def setup_inputs(seed: int = 0) -> dict:
    seeds = jax.random.split(jax.random.key(seed), 8)
    return {
        "layer_input": noise(seeds[0], (N_SECTION, TOKENS, D), 1.0, 6.0, ((0, 8), (1, 16))),
        "resid_grad": noise(seeds[1], (N_SECTION, TOKENS, D), 1.0, 6.0, ((0, 8), (1, 16))),
        "qkv_grad": noise(seeds[2], (N_SECTION, TOKENS, QKV), 1.0, 6.0, ((0, 8), (1, 16))),
        "prev_input": bell_draw_with(seeds[3], (N_SECTION, TOKENS, D), 1.0, 6.0, ((0, 8), (1, 16)), (1, 2, 16, 2.0)),
        "prev_qkv_grad": noise(seeds[4], (N_SECTION, TOKENS, QKV), 0.01, 0.059814453, ((0, 8), (1, 16))),
        "qkv_weight": noise(seeds[5], (N_SECTION, D, QKV), D ** -0.5, 0.125, ((0, 8), (1, 16))),
        "norm_gain": jnp.clip(1.0 + 0.18 * jax.random.normal(seeds[6], (N_SECTION, D), jnp.float32), 0.1, 1.9),
    }


EPS = 1e-05

def row_scale(rows):
    values = rows.astype(jnp.float32)
    return lax.rsqrt(lax.optimization_barrier(jnp.mean(values * values, axis=-1, keepdims=True)) + EPS)

def transpose_product(grads, weight):
    return lax.dot_general(grads, weight, (((1,), (1,)), ((), ())), preferred_element_type=jnp.float32)

def input_backward(rows, resid, grads, weight, gain):
    direction = transpose_product(grads, weight)
    scale = row_scale(rows)
    values = rows.astype(jnp.float32)
    gained = gain[None, :] * direction
    inner = lax.optimization_barrier(jnp.mean(gained * values, axis=-1, keepdims=True))
    result = resid.astype(jnp.float32) + scale * gained - values * scale * scale * scale * inner
    return result.astype(jnp.bfloat16)

def weight_backward(rows, grads, gain):
    scale = row_scale(rows)
    normed = (rows.astype(jnp.float32) * scale * gain[None, :]).astype(jnp.bfloat16)
    normed_blocks = normed.reshape(N_FSDP, TOK_DEV, normed.shape[1])
    grad_blocks = grads.reshape(N_FSDP, TOK_DEV, grads.shape[1])

    def add_block(total, pair):
        term = lax.dot_general(pair[0], pair[1], (((0,), (0,)), ((), ())), preferred_element_type=jnp.float32)
        rounded = lax.optimization_barrier(term.astype(jnp.bfloat16))
        return (total + rounded.astype(jnp.float32), None)
    start = jnp.zeros((normed.shape[1], grads.shape[1]), jnp.float32)
    total, unused = lax.scan(add_block, start, (normed_blocks, grad_blocks))
    return total

def gain_backward(weight_total, weight, gain):
    return lax.optimization_barrier(jnp.sum(weight.astype(jnp.float32) * weight_total, axis=1)) / gain

def reference(layer_input, resid_grad, qkv_grad, prev_input, prev_qkv_grad, qkv_weight, norm_gain):
    locals_list = []
    weight_list = []
    gain_list = []
    for layer in range(N_SECTION):
        locals_list.append(input_backward(layer_input[layer], resid_grad[layer], qkv_grad[layer], qkv_weight[layer], norm_gain[layer]))
        weight_total = weight_backward(prev_input[layer], prev_qkv_grad[layer], norm_gain[layer])
        weight_list.append(weight_total)
        gain_list.append(gain_backward(weight_total, qkv_weight[layer], norm_gain[layer]))
    upstream_grad = jnp.stack(locals_list[1:] + [jnp.zeros_like(locals_list[0])])
    return (upstream_grad, jnp.stack(weight_list), jnp.stack(gain_list))
```

```python
import jax
import jax.numpy as jnp
from jax import lax
from jax.sharding import PartitionSpec as P

EPS = 1e-05


def from_behind(block, axis, distance):
    devices = range(lax.axis_size(axis))
    route = [(i - distance, i) for i in devices if i - distance in devices]
    return lax.ppermute(block, axis, route)


def row_scale(rows):
    values = rows.astype(jnp.float32)
    return lax.rsqrt(jnp.mean(values * values, axis=-1, keepdims=True) + EPS)


def transpose_product(grads, piece):
    return lax.dot_general(
        grads, piece, (((1,), (1,)), ((), ())), preferred_element_type=jnp.float32
    )


def local(layer_input, resid_grad, qkv_grad, prev_input, prev_qkv_grad, qkv_weight, norm_gain):
    rows_now = layer_input[0]
    grads_now = qkv_grad[0]
    rows_prev = prev_input[0]
    grads_prev = prev_qkv_grad[0]
    weight_rows = qkv_weight[0]
    gain = norm_gain[0]
    owned = weight_rows.shape[0]
    prev_scale = row_scale(rows_prev)
    prev_normed = (rows_prev.astype(jnp.float32) * prev_scale * gain[None, :]).astype(jnp.bfloat16)
    direction = transpose_product(
        grads_now, lax.all_gather(weight_rows, "fsdp", axis=0, tiled=True)
    )
    scale = row_scale(rows_now)
    values = rows_now.astype(jnp.float32)
    gained = gain[None, :] * direction
    inner = jnp.mean(gained * values, axis=-1, keepdims=True)
    local_grad = (
        resid_grad[0].astype(jnp.float32) + scale * gained - values * scale * scale * scale * inner
    ).astype(jnp.bfloat16)
    upstream_grad = from_behind(local_grad, "section", -1)
    weight_grad = lax.psum_scatter(
        lax.dot_general(
            prev_normed, grads_prev, (((0,), (0,)), ((), ())), preferred_element_type=jnp.float32
        ).astype(jnp.bfloat16),
        "fsdp",
        scatter_dimension=0,
        tiled=True,
    ).astype(jnp.float32)
    owned_gain = lax.dynamic_slice_in_dim(gain, lax.axis_index("fsdp") * owned, owned, 0)
    gain_part = jnp.sum(weight_rows.astype(jnp.float32) * weight_grad, axis=1) / owned_gain
    gain_grad = lax.all_gather(gain_part, "fsdp", axis=0, tiled=True)
    return (upstream_grad[None], weight_grad[None], gain_grad[None])


def solution(mesh):
    placed = (
        P("section", "fsdp", None),
        P("section", "fsdp", None),
        P("section", "fsdp", None),
        P("section", "fsdp", None),
        P("section", "fsdp", None),
        P("section", "fsdp", None),
        P("section", None),
    )
    return jax.shard_map(
        local,
        mesh=mesh,
        in_specs=placed,
        out_specs=(P("section", "fsdp", None), P("section", "fsdp", None), P("section", None)),
        check_vma=False,
    )
```

```python
import functools

import jax
import jax.numpy as jnp
from jax import lax
from jax.experimental import pallas as pl
from jax.experimental.pallas import tpu as pltpu
from jax.sharding import PartitionSpec as P

EPS = 1e-05
MESH = pl.DeviceIdType.MESH
TOK, D, QKV = 512, 2048, 3072
HALF = TOK // 2
OWN = 128
PIECE = 64
F32, BF16 = jnp.float32, jnp.bfloat16


def kernel(
    x_hbm, res_hbm, q_hbm, prev_hbm, g_hbm, w_hbm, gain_ref,
    up_hbm, wg_hbm, gg_ref,
    w_full, dw, r1, r2, r3, r4, wout, w_own, q_work, normed, n_sib, g_work, g_sib, dirs, x_buf, res_buf, gain_row,
    load_sem, w_sem, ws_sem, tn_sem, tg_sem, tq_sem, sn_sem, sg_sem, rd_sem, r1_sem, r2_sem, r3_sem, r4_sem, lg_sem, gg_sem,
    send_sem, gsend_sem,
):
    s, f = lax.axis_index("section"), lax.axis_index("fsdp")
    c, x, z = s % 2, f // 4, f % 4
    away = (c + x) % 2
    is_away, is_home, has_before = away == 1, away == 0, s > 0

    def at(section, x_to, z_to):
        return (section, ((x_to + 4) % 4) * 4 + (z_to + 4) % 4)

    sib_section = s + 1 - 2 * c
    sibling, across = at(sib_section, x, z), at(s, x + 2, z)
    up, down = at(s, x, z + 1), at(s, x, z - 1)
    left, right = at(sib_section, x - 1, z), at(sib_section, x + 1, z)
    before, after = ((s + 7) % 8, f), ((s + 1) % 8, f)

    sent = []

    def send(make, when=None):
        n = len(sent)

        def build():
            src, dst, recv, device = make()
            return pltpu.make_async_remote_copy(
                src_ref=src, dst_ref=dst, send_sem=send_sem.at[n], recv_sem=recv, device_id=device, device_id_type=MESH
            )

        sent.append([build, when])
        build().start()
        return n

    def wait_sent(n):
        build, when = sent[n]
        if build is None:
            return
        sent[n][0] = None
        if when is None:
            build().wait_send()
        else:
            pl.when(when)(lambda: build().wait_send())

    def load(src, dst, sem):
        copy = pltpu.make_async_copy(src, dst, sem)
        copy.start()
        return copy

    def arrive(dst, sem):
        pltpu.make_async_copy(dst, dst, sem).wait()

    barrier = pltpu.get_barrier_semaphore()

    def greet(device):
        pl.semaphore_signal(barrier, inc=1, device_id=device, device_id_type=MESH)

    @pl.loop(1, 16)
    def _(j):
        greet((s, (f + j) % 16))

    greet(sibling)

    @pl.when(is_away)
    def _():
        greet(left)
        greet(right)

    goes_down = (c == 0) & (s > 0)
    comes_down = (c == 1) & (s < 7)

    @pl.when(goes_down)
    def _():
        greet(before)

    @pl.when(comes_down)
    def _():
        greet(after)

    prev_load = load(prev_hbm, x_buf, load_sem.at[0])
    own_load = load(w_hbm, w_own, load_sem.at[1])
    res_load = load(res_hbm, res_buf, load_sem.at[2])

    pl.semaphore_wait(barrier, 16 + 2 * away + (goes_down | comes_down).astype(jnp.int32))

    def w_piece(k, dz, h, flip=0):
        kind = away if flip == 0 else 1 - away
        xv = x + 2 * k
        owner = (xv + 3 * kind) % 4 if h == 0 else (xv + kind) % 4
        inner = PIECE * kind if h == 0 else PIECE * (1 - kind)
        start = (4 * owner + (z + dz + 4) % 4) * OWN + inner
        return w_full.at[pl.ds(pl.multiple_of(start, PIECE), PIECE)]

    def w_flag(k, dz, h):
        return w_sem.at[8 * ((dz + 4) % 4) + 2 * k + h]

    def ws_flag(k, dz, h):
        return ws_sem.at[8 * ((dz + 4) % 4) + 2 * k + h]

    def to_sibling(k, dz, h):
        send(lambda: (w_piece(k, dz, h), w_piece(k, dz, h), ws_flag(k, dz, h), sibling))

    def to_z(k, dz, h, way):
        send(lambda: (w_piece(k, dz, h), w_piece(k, dz, h), w_flag(k, dz - way, h), up if way == 1 else down))

    def to_column(h):
        send(lambda: (w_piece(0, 0, h), w_piece(0, 0, h), w_flag(1, 0, h), across))

    def spread_own():
        for h in range(2):
            to_column(h)
            to_z(0, 0, h, 1)
            to_z(0, 0, h, -1)
            to_sibling(0, 0, h)

    @pl.when(is_home)
    def _():
        for h in range(2):
            load(w_hbm.at[pl.ds(PIECE * h, PIECE)], w_piece(0, 0, h), w_flag(0, 0, h))
            rows = pl.ds(HALF * h, HALF)
            load(g_hbm.at[rows], g_work.at[rows], tg_sem.at[h])
            load(q_hbm.at[rows], q_work.at[rows], tq_sem.at[h])

    own_rows = pl.multiple_of(f * OWN, OWN)

    @pl.when(is_away)
    def _():
        for h in range(2):

            def own_piece(h=h):
                rows = w_full.at[pl.ds(pl.multiple_of(own_rows + PIECE * h, PIECE), PIECE)]
                return w_hbm.at[pl.ds(PIECE * h, PIECE)], rows, w_flag(0, 0, 1 - h), right if h == 1 else left

            send(own_piece, is_away)

    prev_load.wait()

    @pl.loop(0, TOK // 16)
    def _(i):
        rows = pl.ds(pl.multiple_of(i * 16, 16), 16)
        values = x_buf[rows, :].astype(F32)
        scale = lax.rsqrt(jnp.mean(values * values, axis=-1, keepdims=True) + EPS)
        normed[away, rows, :] = (values * scale * gain_ref[...]).astype(BF16)

    for h in range(2):
        arrive(w_piece(0, 0, h), w_flag(0, 0, h))
    spread_own()
    x_load = load(x_hbm, x_buf, load_sem.at[0])

    def trade(src, dst, sems, h):
        mine, theirs = pl.ds(HALF * h, HALF), pl.ds(HALF * (1 - h), HALF)
        return send(lambda: (src().at[mine], dst().at[theirs], sems(1 - h), left if h == 0 else right), is_away)

    tokens = []

    @pl.when(is_away)
    def _():
        for h in range(2):
            tokens.append(trade(lambda: normed.at[1], lambda: normed.at[0], lambda i: tn_sem.at[i], h))
            tokens.append(trade(lambda: g_hbm, lambda: g_work, lambda i: tg_sem.at[i], h))

    def blocks_of(kind):
        xa = (x + kind) % 4
        return xa, (xa + 2) % 4

    def tokens_to_sibling():
        for j, xb in enumerate(blocks_of(1 - away)):

            def features(j=j, xb=xb):
                columns = pl.ds(pl.multiple_of(512 * xb, 512), 512)
                return normed.at[0, :, columns], n_sib.at[:, pl.ds(512 * j, 512)], sn_sem.at[j], sibling

            send(features)
        send(lambda: (g_work, g_sib, sg_sem, sibling))

    @pl.when(is_home)
    def _():
        for h in range(2):
            arrive(g_work.at[pl.ds(HALF * h, HALF)], tg_sem.at[h])

    for h in range(2):
        arrive(w_piece(1, 0, h), w_flag(1, 0, h))
        to_z(1, 0, h, 1)
        to_z(1, 0, h, -1)
        to_sibling(1, 0, h)
    for k in range(2):
        for h in range(2):
            arrive(w_piece(k, -1, h), w_flag(k, -1, h))
            if h == 0:
                to_z(k, -1, 0, 1)
            arrive(w_piece(k, 1, h), w_flag(k, 1, h))
            if h == 1:
                to_z(k, 1, 1, -1)
            to_sibling(k, -1, h)
            to_sibling(k, 1, h)

    @pl.when(is_away)
    def _():
        for h in range(2):
            arrive(normed.at[0, pl.ds(HALF * h, HALF)], tn_sem.at[h])
            arrive(g_work.at[pl.ds(HALF * h, HALF)], tg_sem.at[h])

    tokens_to_sibling()

    @pl.when(is_away)
    def _():
        for n in tokens:
            wait_sent(n)
        for h in range(2):
            trade(lambda: q_hbm, lambda: q_work, lambda i: tq_sem.at[i], h)

    for j in range(2):
        arrive(n_sib.at[:, pl.ds(512 * j, 512)], sn_sem.at[j])
    arrive(g_sib, sg_sem)
    xa, xb = blocks_of(away)

    def product(dz):
        to = (z + dz) % 4

        def columns(ref, block):
            return ref[:, pl.ds(pl.multiple_of(512 * block + OWN * to, OWN), OWN)]

        mine = jnp.concatenate([columns(normed.at[0], xa), columns(normed.at[0], xb)], axis=1)
        theirs = jnp.concatenate([columns(n_sib, 0), columns(n_sib, 1)], axis=1)

        @pl.loop(0, 4)
        def _(j):
            span = pl.ds(pl.multiple_of(j * 768, 768), 768)
            dims = (((0,), (0,)), ((), ()))
            total = lax.dot_general(mine, g_work[:, span], dims, preferred_element_type=F32)
            total += lax.dot_general(theirs, g_sib[:, span], dims, preferred_element_type=F32)
            dw[dz, :, span] = total.astype(BF16)

    def d_piece(dz, k, h):
        at_home = 128 * k + 64 * h
        at_away = 128 * k if h == 1 else 192 - 128 * k
        return dw.at[dz, pl.ds(pl.multiple_of(at_home + away * (at_away - at_home), PIECE), PIECE)]

    product(2)
    first = []
    for k in (1, 0):
        first.append(send(lambda k=k: (d_piece(2, k, 0), r1.at[0, k], r1_sem.at[k], up)))
        first.append(send(lambda k=k: (d_piece(2, k, 1), r1.at[1, k], r1_sem.at[2 + k], down)))
    product(1)
    product(3)
    product(0)

    for k in range(2):
        for h in range(2):
            arrive(w_piece(k, 2, h), w_flag(k, 2, h))
            to_sibling(k, 2, h)

    def to_next(k, h, way):
        dz, side = (1, 0) if way == 1 else (3, 1)
        send(lambda: (d_piece(dz, k, h), r2.at[side, k, h], r2_sem.at[4 * side + 2 * k + h], up if way == 1 else down))

    for n in first[:2]:
        wait_sent(n)
    for k in (1, 0):
        to_next(k, 1, 1)
        to_next(k, 0, -1)

    for h in range(2):
        arrive(q_work.at[pl.ds(HALF * h, HALF)], tq_sem.at[h])
    for dz in range(4):
        for k in range(2):
            for h in range(2):
                arrive(w_piece(k, dz, h, 1), ws_flag(k, dz, h))

    for block in range(4):

        @pl.loop(0, 2)
        def _(j):
            rows = pl.ds(pl.multiple_of(512 * block + 256 * j, 256), 256)
            out = lax.dot_general(q_work[...], w_full[rows, :], (((1,), (1,)), ((), ())), preferred_element_type=F32)
            dirs[0, :, rows] = out.astype(BF16)

        @pl.when(is_away)
        def _():
            columns = pl.ds(512 * block, 512)
            for h in range(2):
                flags = functools.partial(lambda block, i: rd_sem.at[i, block], block)
                trade(lambda: dirs.at[0, :, columns], lambda: dirs.at[1, :, columns], flags, h)

    def add_into(target, term):
        @pl.loop(0, QKV // 512)
        def _(j):
            span = pl.ds(pl.multiple_of(j * 512, 512), 512)
            target[:, span] = (target[:, span].astype(F32) + term[:, span].astype(F32)).astype(BF16)

    for k in (1, 0):
        arrive(r1.at[0, k], r1_sem.at[k])
        add_into(d_piece(1, k, 0), r1.at[0, k])
        to_next(k, 0, 1)
        arrive(r1.at[1, k], r1_sem.at[2 + k])
        add_into(d_piece(3, k, 1), r1.at[1, k])
        to_next(k, 1, -1)

    @pl.when(is_away)
    def _():
        for h in range(2):
            for block in range(4):
                arrive(dirs.at[1, pl.ds(HALF * h, HALF), pl.ds(512 * block, 512)], rd_sem.at[h, block])

    x_load.wait()
    res_load.wait()
    for part in range(4):

        @pl.loop(0, 8)
        def _(i):
            rows = pl.ds(pl.multiple_of(128 * part + i * 16, 16), 16)
            values = x_buf[rows, :].astype(F32)
            scale = lax.rsqrt(jnp.mean(values * values, axis=-1, keepdims=True) + EPS)
            gained = gain_ref[...] * dirs[away, rows, :].astype(F32)
            inner = jnp.mean(gained * values, axis=-1, keepdims=True)
            out = res_buf[rows, :].astype(F32) + scale * gained - values * (scale * scale * scale * inner)
            res_buf[rows, :] = out.astype(BF16)

        @pl.when(has_before)
        def _():
            rows = pl.ds(128 * part, 128)
            send(lambda part=part: (res_buf.at[rows], up_hbm.at[rows], lg_sem.at[part], before), has_before)

    def sum_into(target, k, h):
        @pl.loop(0, QKV // 512)
        def _(j):
            span = pl.ds(pl.multiple_of(j * 512, 512), 512)
            total = target[:, span].astype(F32) + r2[0, k, h, :, span].astype(F32) + r2[1, k, h, :, span].astype(F32)
            target[:, span] = total.astype(BF16)

    def r2_arrive(k, h):
        arrive(r2.at[0, k, h], r2_sem.at[2 * k + h])
        arrive(r2.at[1, k, h], r2_sem.at[4 + 2 * k + h])

    for h in range(2):
        r2_arrive(1, h)
        sum_into(d_piece(0, 1, h), 1, h)
        send(lambda h=h: (d_piece(0, 1, h), r3.at[h], r3_sem.at[h], across))

    own_load.wait()
    for h in range(2):
        r2_arrive(0, h)
        arrive(r3.at[h], r3_sem.at[h])
        target = d_piece(0, 0, h)

        @pl.loop(0, QKV // 512)
        def _(j):
            span = pl.ds(pl.multiple_of(j * 512, 512), 512)
            total = target[:, span].astype(F32) + r2[0, 0, h, :, span].astype(F32) + r2[1, 0, h, :, span].astype(F32)
            total += r3[h, :, span].astype(F32)
            wout[pl.ds(PIECE * h, PIECE), span] = total
            target[:, span] = total.astype(BF16)

        @pl.when(is_away)
        def _():
            send(lambda h=h: (d_piece(0, 0, h), r4.at[1 - h], r4_sem.at[1 - h], left if h == 0 else right), is_away)

    @pl.when(is_away)
    def _():
        for h in range(2):
            arrive(r4.at[h], r4_sem.at[h])

            @pl.loop(0, QKV // 512)
            def _(j):
                span = pl.ds(pl.multiple_of(j * 512, 512), 512)
                wout[pl.ds(PIECE * h, PIECE), span] = r4[h, :, span].astype(F32)

    w_store = load(wout, wg_hbm, load_sem.at[3])

    def fold(i, total):
        span = pl.ds(pl.multiple_of(i * 128, 128), 128)
        return total + w_own[:, span].astype(F32) * wout[:, span]

    folded = lax.fori_loop(0, QKV // 128, fold, jnp.zeros((OWN, 128), F32))
    part = jnp.sum(folded.T, axis=0, keepdims=True) / gain_ref[:, pl.ds(own_rows, OWN)]
    gain_row[...] = part
    gg_ref[f, :, :] = part

    def gain_copy(j, source):
        return pltpu.make_async_remote_copy(
            src_ref=gain_row, dst_ref=gg_ref.at[source], send_sem=gsend_sem.at[j], recv_sem=gg_sem.at[source],
            device_id=(s, (f + j) % 16), device_id_type=MESH,
        )

    @pl.loop(1, 16)
    def _(j):
        gain_copy(j, f).start()

    @pl.when(s < 7)
    def _():
        for part in range(4):
            rows = pl.ds(128 * part, 128)
            arrive(up_hbm.at[rows], lg_sem.at[part])

    @pl.loop(1, 16)
    def _(j):
        source = (f + 16 - j) % 16
        gain_copy(j, source).wait_recv()
        gain_copy(j, f).wait_send()

    w_store.wait()
    for n in range(len(sent)):
        wait_sent(n)


SENDS = 120


def local(layer_input, resid_grad, qkv_grad, prev_input, prev_qkv_grad, qkv_weight, norm_gain):
    hbm = pl.BlockSpec(memory_space=pl.ANY)
    vmem = pl.BlockSpec(memory_space=pltpu.VMEM)
    dma = pltpu.SemaphoreType.DMA
    received, weight_grad, gain_rows = pl.pallas_call(
        kernel,
        out_shape=(
            jax.ShapeDtypeStruct((TOK, D), BF16),
            jax.ShapeDtypeStruct((OWN, QKV), F32),
            jax.ShapeDtypeStruct((16, 1, OWN), F32),
        ),
        in_specs=[hbm] * 6 + [vmem],
        out_specs=(hbm, hbm, vmem),
        scratch_shapes=[
            pltpu.VMEM((D, QKV), BF16),
            pltpu.VMEM((4, 256, QKV), BF16),
            pltpu.VMEM((2, 2, PIECE, QKV), BF16),
            pltpu.VMEM((2, 2, 2, PIECE, QKV), BF16),
            pltpu.VMEM((2, PIECE, QKV), BF16),
            pltpu.VMEM((2, PIECE, QKV), BF16),
            pltpu.VMEM((OWN, QKV), F32),
            pltpu.VMEM((OWN, QKV), BF16),
            pltpu.VMEM((TOK, QKV), BF16),
            pltpu.VMEM((2, TOK, D), BF16),
            pltpu.VMEM((TOK, D // 2), BF16),
            pltpu.VMEM((TOK, QKV), BF16),
            pltpu.VMEM((TOK, QKV), BF16),
            pltpu.VMEM((2, TOK, D), BF16),
            pltpu.VMEM((TOK, D), BF16),
            pltpu.VMEM((TOK, D), BF16),
            pltpu.VMEM((1, OWN), F32),
            dma((4,)),
            dma((32,)),
            dma((32,)),
            dma((2,)),
            dma((2,)),
            dma((2,)),
            dma((2,)),
            dma(()),
            dma((2, 4)),
            dma((4,)),
            dma((8,)),
            dma((2,)),
            dma((2,)),
            dma((4,)),
            dma((16,)),
            dma((SENDS,)),
            dma((16,)),
        ],
        compiler_params=pltpu.CompilerParams(collective_id=0, has_side_effects=True, vmem_limit_bytes=62 << 20),
    )(layer_input[0], resid_grad[0], qkv_grad[0], prev_input[0], prev_qkv_grad[0], qkv_weight[0], norm_gain)
    last = lax.axis_index("section") == lax.axis_size("section") - 1
    upstream_grad = jnp.where(last, jnp.zeros_like(received), received)
    return (upstream_grad[None], weight_grad[None], gain_rows.reshape(1, D))


def solution(mesh):
    tokens, whole = P("section", "fsdp", None), P("section", None)
    return jax.shard_map(
        local,
        mesh=mesh,
        in_specs=(tokens,) * 6 + (whole,),
        out_specs=(tokens, tokens, whole),
        check_vma=False,
    )
```

```python
import functools

import jax
import jax.numpy as jnp
from jax import lax
from jax.experimental import pallas as pl
from jax.experimental.pallas import tpu as pltpu
from jax.sharding import PartitionSpec as P

EPS = 1e-05
MESH = pl.DeviceIdType.MESH
TOK, D, QKV = 512, 2048, 3072
HALF = TOK // 2
CHUNK = HALF // 2
OWN = 128
PIECE = 64
F32, BF16 = jnp.float32, jnp.bfloat16


def kernel(
    x_hbm, res_hbm, q_hbm, prev_hbm, g_hbm, w_hbm, gain_ref,
    up_hbm, wg_hbm, gg_ref,
    w_full, dw, r1, r2, r3, r4, wout, q_work, normed, n_sib, g_work, g_sib, dirs, x_buf, res_buf, gain_part, gain_sib, gain_all,
    load_sem, w_sem, ws_sem, tn_sem, tg_sem, tq_sem, sn_sem, sg_sem, rd_sem, r1_sem, r2_sem, r3_sem, r4_sem, lg_sem, gp_sem, gg_sem,
    send_sem, gsend_sem,
):
    s, f = lax.axis_index("section"), lax.axis_index("fsdp")
    c, x, z = s % 2, f // 4, f % 4
    away = (c + x) % 2
    is_away, is_home, has_before = away == 1, away == 0, s > 0

    def at(section, x_to, z_to):
        return (section, ((x_to + 4) % 4) * 4 + (z_to + 4) % 4)

    sib_section = s + 1 - 2 * c
    sibling, across = at(sib_section, x, z), at(s, x + 2, z)
    up, down = at(s, x, z + 1), at(s, x, z - 1)
    left, right = at(sib_section, x - 1, z), at(sib_section, x + 1, z)
    before, after = ((s + 7) % 8, f), ((s + 1) % 8, f)

    sent = []

    def send(make, when=None):
        n = len(sent)

        def build():
            src, dst, recv, device = make()
            return pltpu.make_async_remote_copy(
                src_ref=src, dst_ref=dst, send_sem=send_sem.at[n], recv_sem=recv, device_id=device, device_id_type=MESH
            )

        sent.append([build, when])
        build().start()
        return n

    def wait_sent(n):
        build, when = sent[n]
        if build is None:
            return
        sent[n][0] = None
        if when is None:
            build().wait_send()
        else:
            pl.when(when)(lambda: build().wait_send())

    def load(src, dst, sem):
        copy = pltpu.make_async_copy(src, dst, sem)
        copy.start()
        return copy

    def arrive(dst, sem):
        pltpu.make_async_copy(dst, dst, sem).wait()

    barrier = pltpu.get_barrier_semaphore()

    def greet(device):
        pl.semaphore_signal(barrier, inc=1, device_id=device, device_id_type=MESH)

    @pl.loop(1, 16)
    def _(j):
        greet((s, (f + j) % 16))

    greet(sibling)

    @pl.when(is_away)
    def _():
        greet(left)
        greet(right)

    goes_down = (c == 0) & (s > 0)
    comes_down = (c == 1) & (s < 7)

    @pl.when(goes_down)
    def _():
        greet(before)

    @pl.when(comes_down)
    def _():
        greet(after)

    pl.semaphore_wait(barrier, 16 + 2 * away + (goes_down | comes_down).astype(jnp.int32))

    def w_piece(k, dz, h, flip=0):
        kind = away if flip == 0 else 1 - away
        xv = x + 2 * k
        owner = (xv + 3 * kind) % 4 if h == 0 else (xv + kind) % 4
        inner = PIECE * kind if h == 0 else PIECE * (1 - kind)
        start = (4 * owner + (z + dz + 4) % 4) * OWN + inner
        return w_full.at[pl.ds(pl.multiple_of(start, PIECE), PIECE)]

    def w_flag(k, dz, h):
        return w_sem.at[8 * ((dz + 4) % 4) + 2 * k + h]

    def ws_flag(k, dz, h):
        return ws_sem.at[8 * ((dz + 4) % 4) + 2 * k + h]

    def to_sibling(k, dz, h):
        send(lambda: (w_piece(k, dz, h), w_piece(k, dz, h), ws_flag(k, dz, h), sibling))

    def to_z(k, dz, h, way):
        send(lambda: (w_piece(k, dz, h), w_piece(k, dz, h), w_flag(k, dz - way, h), up if way == 1 else down))

    def own_across(source, when):
        for h in range(2):
            send(lambda h=h: (source(h), w_piece(0, 0, h), w_flag(1, 0, h), across), when)

    def spread_own(source, when):
        for h in range(2):
            send(lambda h=h: (source(h), w_piece(0, 0, h), w_flag(0, -1, h), up), when)
            send(lambda h=h: (source(h), w_piece(0, 0, h), w_flag(0, 1, h), down), when)
        for h in range(2):
            send(lambda h=h: (source(h), w_piece(0, 0, h), ws_flag(0, 0, h), sibling), when)

    def half_rows(h):
        return w_hbm.at[pl.ds(PIECE * h, PIECE)]

    @pl.when(is_home)
    def _():
        spread_own(half_rows, is_home)
        for h in range(2):
            load(half_rows(h), w_piece(0, 0, h), w_flag(0, 0, h))

    own_rows = pl.multiple_of(f * OWN, OWN)

    @pl.when(is_away)
    def _():
        for h in range(2):

            def own_piece(h=h):
                rows = w_full.at[pl.ds(pl.multiple_of(own_rows + PIECE * h, PIECE), PIECE)]
                return half_rows(h), rows, w_flag(0, 0, 1 - h), right if h == 1 else left

            send(own_piece, is_away)

    prev_load = load(prev_hbm, x_buf, load_sem.at[0])
    res_load = load(res_hbm, res_buf, load_sem.at[2])

    def chunk(h, i):
        return pl.ds(HALF * h + CHUNK * i, CHUNK)

    def whole(h):
        return pl.ds(HALF * h, HALF)

    def trade(src, dst, flag, h, rows=whole):
        send(lambda: (src().at[rows(h)], dst().at[rows(1 - h)], flag(1 - h), left if h == 0 else right), is_away)

    def trade_g(i):
        for h in range(2):
            trade(lambda: g_hbm, lambda: g_work, lambda h: tg_sem.at[h, i], h, lambda h: chunk(h, i))

    def g_to_sibling(source, i, when):
        for h in range(2):
            send(lambda h=h: (source.at[chunk(h, i)], g_sib.at[chunk(h, i)], sg_sem.at[h, i], sibling), when)

    @pl.when(is_home)
    def _():
        for h in range(2):
            for i in range(2):
                load(g_hbm.at[chunk(h, i)], g_work.at[chunk(h, i)], tg_sem.at[h, i])
            load(q_hbm.at[whole(h)], q_work.at[whole(h)], tq_sem.at[h])

    prev_load.wait()

    @pl.loop(0, TOK // 16)
    def _(i):
        rows = pl.ds(pl.multiple_of(i * 16, 16), 16)
        values = x_buf[rows, :].astype(F32)
        scale = lax.rsqrt(jnp.mean(values * values, axis=-1, keepdims=True) + EPS)
        normed[away, rows, :] = (values * scale * gain_ref[...]).astype(BF16)

    def blocks_of(kind):
        xa = (x + kind) % 4
        return xa, (xa + 2) % 4

    sib_blocks = blocks_of(1 - away)

    def n_to_sibling(when):
        for j, block in enumerate(sib_blocks):

            def features(j=j, block=block):
                columns = pl.ds(pl.multiple_of(512 * block, 512), 512)
                return normed.at[0, :, columns], n_sib.at[:, pl.ds(512 * j, 512)], sn_sem.at[j], sibling

            send(features, when)

    for h in range(2):
        arrive(w_piece(0, 0, h), w_flag(0, 0, h))

    @pl.when(is_away)
    def _():
        own_across(lambda h: w_piece(0, 0, h), is_away)
        spread_own(lambda h: w_piece(0, 0, h), is_away)
        for h in range(2):
            trade(lambda: normed.at[1], lambda: normed.at[0], lambda h: tn_sem.at[h], h)

    @pl.when(is_home)
    def _():
        own_across(half_rows, is_home)
        n_to_sibling(is_home)
        for i in range(2):
            g_to_sibling(g_hbm, i, is_home)

    x_load = load(x_hbm, x_buf, load_sem.at[0])

    for h in range(2):
        arrive(w_piece(1, 0, h), w_flag(1, 0, h))
        to_z(1, 0, h, 1)
        to_z(1, 0, h, -1)
        to_sibling(1, 0, h)

    @pl.when(is_away)
    def _():
        trade_g(0)

    def pass_on(k):
        for h in range(2):
            arrive(w_piece(k, -1, h), w_flag(k, -1, h))
            if h == 0:
                to_z(k, -1, 0, 1)
            arrive(w_piece(k, 1, h), w_flag(k, 1, h))
            if h == 1:
                to_z(k, 1, 1, -1)
            to_sibling(k, -1, h)
            to_sibling(k, 1, h)

    pass_on(0)

    @pl.when(is_away)
    def _():
        trade_g(1)
        for h in range(2):
            arrive(normed.at[0, whole(h)], tn_sem.at[h])
        n_to_sibling(is_away)

    def pass_g(i):
        for h in range(2):
            arrive(g_work.at[chunk(h, i)], tg_sem.at[h, i])

        @pl.when(is_away)
        def _():
            g_to_sibling(g_work, i, is_away)

    pass_g(0)
    pass_on(1)
    pass_g(1)


    @pl.when(is_away)
    def _():
        for h in range(2):
            trade(lambda: q_hbm, lambda: q_work, lambda h: tq_sem.at[h], h)

    for j in range(2):
        arrive(n_sib.at[:, pl.ds(512 * j, 512)], sn_sem.at[j])
    for i in range(2):
        for h in range(2):
            arrive(g_sib.at[chunk(h, i)], sg_sem.at[h, i])
    xa, xb = blocks_of(away)

    def product(dz):
        to = (z + dz) % 4

        def columns(ref, block):
            return ref[:, pl.ds(pl.multiple_of(512 * block + OWN * to, OWN), OWN)]

        mine = jnp.concatenate([columns(normed.at[0], xa), columns(normed.at[0], xb)], axis=1)
        theirs = jnp.concatenate([columns(n_sib, 0), columns(n_sib, 1)], axis=1)

        @pl.loop(0, 4)
        def _(j):
            span = pl.ds(pl.multiple_of(j * 768, 768), 768)
            dims = (((0,), (0,)), ((), ()))
            total = lax.dot_general(mine, g_work[:, span], dims, preferred_element_type=F32)
            total += lax.dot_general(theirs, g_sib[:, span], dims, preferred_element_type=F32)
            dw[dz, :, span] = total.astype(BF16)

    def d_piece(dz, k, h):
        at_home = 128 * k + 64 * h
        at_away = 128 * k if h == 1 else 192 - 128 * k
        return dw.at[dz, pl.ds(pl.multiple_of(at_home + away * (at_away - at_home), PIECE), PIECE)]

    product(2)
    first = []
    for k in (1, 0):
        first.append(send(lambda k=k: (d_piece(2, k, 0), r1.at[0, k], r1_sem.at[k], up)))
        first.append(send(lambda k=k: (d_piece(2, k, 1), r1.at[1, k], r1_sem.at[2 + k], down)))

    for k in range(2):
        for h in range(2):
            arrive(w_piece(k, 2, h), w_flag(k, 2, h))
            to_sibling(k, 2, h)

    product(1)
    product(3)

    def to_next(k, h, way):
        dz, side = (1, 0) if way == 1 else (3, 1)
        send(lambda: (d_piece(dz, k, h), r2.at[side, k, h], r2_sem.at[4 * side + 2 * k + h], up if way == 1 else down))

    def add_into(target, term):
        @pl.loop(0, QKV // 512)
        def _(j):
            span = pl.ds(pl.multiple_of(j * 512, 512), 512)
            target[:, span] = (target[:, span].astype(F32) + term[:, span].astype(F32)).astype(BF16)

    def direct(k):
        to_next(k, 1, 1)
        to_next(k, 0, -1)

    def summed(k):
        arrive(r1.at[0, k], r1_sem.at[k])
        add_into(d_piece(1, k, 0), r1.at[0, k])
        to_next(k, 0, 1)
        arrive(r1.at[1, k], r1_sem.at[2 + k])
        add_into(d_piece(3, k, 1), r1.at[1, k])
        to_next(k, 1, -1)

    for n in first[:2]:
        wait_sent(n)
    direct(1)
    product(0)

    def gain_copy(j, source):
        return pltpu.make_async_remote_copy(
            src_ref=gain_all.at[source], dst_ref=gain_all.at[source], send_sem=gsend_sem.at[j], recv_sem=gg_sem.at[source],
            device_id=(s, (f + j) % 16), device_id_type=MESH,
        )

    for dz in range(4):
        for k in range(2):
            for h in range(2):
                arrive(w_piece(k, dz, h, 1), ws_flag(k, dz, h))

    @pl.loop(0, D // 256)
    def _(j):
        rows = pl.ds(pl.multiple_of(256 * j, 256), 256)
        out = lax.dot_general(g_work[...], w_full[rows, :], (((1,), (1,)), ((), ())), preferred_element_type=F32)
        gain_part[:, rows] = jnp.sum(out * normed[0, :, rows].astype(F32), axis=0, keepdims=True)

    slot = 4 * (x // 2) + z

    @pl.when(is_away)
    def _():
        send(lambda: (gain_part, gain_sib, gp_sem, sibling), is_away)

    @pl.when(is_home)
    def _():
        arrive(gain_sib, gp_sem)
        gain_all[slot, :, :] = gain_part[...] + gain_sib[...]

        @pl.loop(1, 16)
        def _(j):
            gain_copy(j, slot).start()

    for h in range(2):
        arrive(q_work.at[whole(h)], tq_sem.at[h])

    def direction(block):
        @pl.loop(0, 2)
        def _(j):
            rows = pl.ds(pl.multiple_of(512 * block + 256 * j, 256), 256)
            out = lax.dot_general(q_work[...], w_full[rows, :], (((1,), (1,)), ((), ())), preferred_element_type=F32)
            dirs[0, :, rows] = out.astype(BF16)

        @pl.when(is_away)
        def _():
            columns = pl.ds(512 * block, 512)
            for h in range(2):
                trade(lambda: dirs.at[0, :, columns], lambda: dirs.at[1, :, columns], lambda h: rd_sem.at[h, block], h)

    direction(0)
    direction(1)
    for n in first[2:]:
        wait_sent(n)
    summed(1)
    direct(0)
    direction(2)
    direction(3)
    summed(0)

    @pl.when(is_away)
    def _():
        for h in range(2):
            for block in range(4):
                arrive(dirs.at[1, whole(h), pl.ds(512 * block, 512)], rd_sem.at[h, block])

    x_load.wait()
    res_load.wait()
    for part in range(4):

        @pl.loop(0, 8)
        def _(i):
            rows = pl.ds(pl.multiple_of(128 * part + i * 16, 16), 16)
            values = x_buf[rows, :].astype(F32)
            scale = lax.rsqrt(jnp.mean(values * values, axis=-1, keepdims=True) + EPS)
            gained = gain_ref[...] * dirs[away, rows, :].astype(F32)
            inner = jnp.mean(gained * values, axis=-1, keepdims=True)
            out = res_buf[rows, :].astype(F32) + scale * gained - values * (scale * scale * scale * inner)
            res_buf[rows, :] = out.astype(BF16)

        @pl.when(has_before)
        def _():
            rows = pl.ds(128 * part, 128)
            send(lambda part=part: (res_buf.at[rows], up_hbm.at[rows], lg_sem.at[part], before), has_before)

    def sum_into(target, k, h):
        @pl.loop(0, QKV // 512)
        def _(j):
            span = pl.ds(pl.multiple_of(j * 512, 512), 512)
            total = target[:, span].astype(F32) + r2[0, k, h, :, span].astype(F32) + r2[1, k, h, :, span].astype(F32)
            target[:, span] = total.astype(BF16)

    def r2_arrive(k, h):
        arrive(r2.at[0, k, h], r2_sem.at[2 * k + h])
        arrive(r2.at[1, k, h], r2_sem.at[4 + 2 * k + h])

    for h in range(2):
        r2_arrive(1, h)
        sum_into(d_piece(0, 1, h), 1, h)
        send(lambda h=h: (d_piece(0, 1, h), r3.at[h], r3_sem.at[h], across))

    for h in range(2):
        r2_arrive(0, h)
        arrive(r3.at[h], r3_sem.at[h])
        target = d_piece(0, 0, h)

        @pl.loop(0, QKV // 512)
        def _(j):
            span = pl.ds(pl.multiple_of(j * 512, 512), 512)
            total = target[:, span].astype(F32) + r2[0, 0, h, :, span].astype(F32) + r2[1, 0, h, :, span].astype(F32)
            total += r3[h, :, span].astype(F32)
            wout[pl.ds(PIECE * h, PIECE), span] = total
            target[:, span] = total.astype(BF16)

        @pl.when(is_away)
        def _():
            send(lambda h=h: (d_piece(0, 0, h), r4.at[1 - h], r4_sem.at[1 - h], left if h == 0 else right), is_away)

    @pl.when(is_away)
    def _():
        for h in range(2):
            arrive(r4.at[h], r4_sem.at[h])

            @pl.loop(0, QKV // 512)
            def _(j):
                span = pl.ds(pl.multiple_of(j * 512, 512), 512)
                wout[pl.ds(PIECE * h, PIECE), span] = r4[h, :, span].astype(F32)

    w_store = load(wout, wg_hbm, load_sem.at[3])

    for j in range(8):

        @pl.when(is_away | (slot != j))
        def _():
            arrive(gain_all.at[j], gg_sem.at[j])

    gg_ref[...] = jnp.sum(gain_all[...], axis=0) / gain_ref[...]

    @pl.when(s < 7)
    def _():
        for part in range(4):
            rows = pl.ds(128 * part, 128)
            arrive(up_hbm.at[rows], lg_sem.at[part])

    @pl.when(is_home)
    def _():
        @pl.loop(1, 16)
        def _(j):
            gain_copy(j, slot).wait_send()

    w_store.wait()
    for n in range(len(sent)):
        wait_sent(n)


SENDS = 128


def local(layer_input, resid_grad, qkv_grad, prev_input, prev_qkv_grad, qkv_weight, norm_gain):
    hbm = pl.BlockSpec(memory_space=pl.ANY)
    vmem = pl.BlockSpec(memory_space=pltpu.VMEM)
    dma = pltpu.SemaphoreType.DMA
    received, weight_grad, gain_grad = pl.pallas_call(
        kernel,
        out_shape=(
            jax.ShapeDtypeStruct((TOK, D), BF16),
            jax.ShapeDtypeStruct((OWN, QKV), F32),
            jax.ShapeDtypeStruct((1, D), F32),
        ),
        in_specs=[hbm] * 6 + [vmem],
        out_specs=(hbm, hbm, vmem),
        scratch_shapes=[
            pltpu.VMEM((D, QKV), BF16),
            pltpu.VMEM((4, 256, QKV), BF16),
            pltpu.VMEM((2, 2, PIECE, QKV), BF16),
            pltpu.VMEM((2, 2, 2, PIECE, QKV), BF16),
            pltpu.VMEM((2, PIECE, QKV), BF16),
            pltpu.VMEM((2, PIECE, QKV), BF16),
            pltpu.VMEM((OWN, QKV), F32),
            pltpu.VMEM((TOK, QKV), BF16),
            pltpu.VMEM((2, TOK, D), BF16),
            pltpu.VMEM((TOK, D // 2), BF16),
            pltpu.VMEM((TOK, QKV), BF16),
            pltpu.VMEM((TOK, QKV), BF16),
            pltpu.VMEM((2, TOK, D), BF16),
            pltpu.VMEM((TOK, D), BF16),
            pltpu.VMEM((TOK, D), BF16),
            pltpu.VMEM((1, D), F32),
            pltpu.VMEM((1, D), F32),
            pltpu.VMEM((8, 1, D), F32),
            dma((4,)),
            dma((32,)),
            dma((32,)),
            dma((2,)),
            dma((2, 2)),
            dma((2,)),
            dma((2,)),
            dma((2, 2)),
            dma((2, 4)),
            dma((4,)),
            dma((8,)),
            dma((2,)),
            dma((2,)),
            dma((4,)),
            dma(()),
            dma((8,)),
            dma((SENDS,)),
            dma((16,)),
        ],
        compiler_params=pltpu.CompilerParams(collective_id=0, has_side_effects=True, vmem_limit_bytes=62 << 20),
    )(layer_input[0], resid_grad[0], qkv_grad[0], prev_input[0], prev_qkv_grad[0], qkv_weight[0], norm_gain)
    last = lax.axis_index("section") == lax.axis_size("section") - 1
    upstream_grad = jnp.where(last, jnp.zeros_like(received), received)
    return (upstream_grad[None], weight_grad[None], gain_grad)


def solution(mesh):
    tokens, whole = P("section", "fsdp", None), P("section", None)
    return jax.shard_map(
        local,
        mesh=mesh,
        in_specs=(tokens,) * 6 + (whole,),
        out_specs=(tokens, tokens, whole),
        check_vma=False,
    )
```

```python
import functools

import jax
import jax.numpy as jnp
from jax import lax
from jax.experimental import pallas as pl
from jax.experimental.pallas import tpu as pltpu
from jax.sharding import PartitionSpec as P

EPS = 1e-05
MESH = pl.DeviceIdType.MESH
TOK, D, QKV = 512, 2048, 3072
HALF = TOK // 2
CHUNK = HALF // 2
OWN = 128
PIECE = 64
F32, BF16 = jnp.float32, jnp.bfloat16


def kernel(
    x_hbm, res_hbm, q_hbm, prev_hbm, g_hbm, w_hbm, gain_ref,
    up_hbm, wg_hbm, gg_ref,
    w_full, dw, r1, r2, r3, r4, wout, q_work, normed, n_sib, g_work, g_sib, dirs, x_buf, res_buf, gain_part, gain_sib, gain_all,
    load_sem, w_sem, ws_sem, tn_sem, tg_sem, tq_sem, sn_sem, sg_sem, rd_sem, r1_sem, r2_sem, r3_sem, r4_sem, lg_sem, gp_sem, gg_sem,
    send_sem, gsend_sem,
):
    s, f = lax.axis_index("section"), lax.axis_index("fsdp")
    c, x, z = s % 2, f // 4, f % 4
    away = (c + x) % 2
    is_away, is_home, has_before = away == 1, away == 0, s > 0

    def at(section, x_to, z_to):
        return (section, ((x_to + 4) % 4) * 4 + (z_to + 4) % 4)

    sib_section = s + 1 - 2 * c
    sibling, across = at(sib_section, x, z), at(s, x + 2, z)
    up, down = at(s, x, z + 1), at(s, x, z - 1)
    left, right = at(sib_section, x - 1, z), at(sib_section, x + 1, z)
    before, after = ((s + 7) % 8, f), ((s + 1) % 8, f)

    sent = []

    def send(make, when=None):
        n = len(sent)

        def build():
            src, dst, recv, device = make()
            return pltpu.make_async_remote_copy(
                src_ref=src, dst_ref=dst, send_sem=send_sem.at[n], recv_sem=recv, device_id=device, device_id_type=MESH
            )

        sent.append([build, when])
        build().start()
        return n

    def wait_sent(n):
        build, when = sent[n]
        if build is None:
            return
        sent[n][0] = None
        if when is None:
            build().wait_send()
        else:
            pl.when(when)(lambda: build().wait_send())

    def load(src, dst, sem):
        copy = pltpu.make_async_copy(src, dst, sem)
        copy.start()
        return copy

    def arrive(dst, sem):
        pltpu.make_async_copy(dst, dst, sem).wait()

    barrier = pltpu.get_barrier_semaphore()

    def greet(device):
        pl.semaphore_signal(barrier, inc=1, device_id=device, device_id_type=MESH)

    @pl.loop(1, 16)
    def _(j):
        greet((s, (f + j) % 16))

    greet(sibling)

    @pl.when(is_away)
    def _():
        greet(left)
        greet(right)

    goes_down = (c == 0) & (s > 0)
    comes_down = (c == 1) & (s < 7)

    @pl.when(goes_down)
    def _():
        greet(before)

    @pl.when(comes_down)
    def _():
        greet(after)

    pl.semaphore_wait(barrier, 16 + 2 * away + (goes_down | comes_down).astype(jnp.int32))

    def w_piece(k, dz, h, flip=0):
        kind = away if flip == 0 else 1 - away
        xv = x + 2 * k
        owner = (xv + 3 * kind) % 4 if h == 0 else (xv + kind) % 4
        inner = PIECE * kind if h == 0 else PIECE * (1 - kind)
        start = (4 * owner + (z + dz + 4) % 4) * OWN + inner
        return w_full.at[pl.ds(pl.multiple_of(start, PIECE), PIECE)]

    def w_flag(k, dz, h):
        return w_sem.at[8 * ((dz + 4) % 4) + 2 * k + h]

    def ws_flag(k, dz, h):
        return ws_sem.at[8 * ((dz + 4) % 4) + 2 * k + h]

    def to_sibling(k, dz, h, when=None):
        send(lambda: (w_piece(k, dz, h), w_piece(k, dz, h), ws_flag(k, dz, h), sibling), when)

    def to_z(k, dz, h, way, when=None):
        send(lambda: (w_piece(k, dz, h), w_piece(k, dz, h), w_flag(k, dz - way, h), up if way == 1 else down), when)

    def own_across(source, when):
        for h in range(2):
            send(lambda h=h: (source(h), w_piece(0, 0, h), w_flag(1, 0, h), across), when)

    def spread_own(source, when):
        for h in range(2):
            send(lambda h=h: (source(h), w_piece(0, 0, h), w_flag(0, -1, h), up), when)
            send(lambda h=h: (source(h), w_piece(0, 0, h), w_flag(0, 1, h), down), when)
        for h in range(2):
            send(lambda h=h: (source(h), w_piece(0, 0, h), ws_flag(0, 0, h), sibling), when)

    def half_rows(h):
        return w_hbm.at[pl.ds(PIECE * h, PIECE)]

    @pl.when(is_home)
    def _():
        spread_own(half_rows, is_home)
        for h in range(2):
            load(half_rows(h), w_piece(0, 0, h), w_flag(0, 0, h))

    own_rows = pl.multiple_of(f * OWN, OWN)

    @pl.when(is_away)
    def _():
        for k in range(2):
            for h in range(2):

                def own_piece(k=k, h=h):
                    rows = w_full.at[pl.ds(pl.multiple_of(own_rows + PIECE * h, PIECE), PIECE)]
                    return half_rows(h), rows, w_flag(k, 0, 1 - h), right if h != k else left

                send(own_piece, is_away)

    prev_load = load(prev_hbm, x_buf, load_sem.at[0])
    res_load = load(res_hbm, res_buf, load_sem.at[2])

    def chunk(h, i):
        return pl.ds(HALF * h + CHUNK * i, CHUNK)

    def whole(h):
        return pl.ds(HALF * h, HALF)

    def trade(src, dst, flag, h, rows=whole):
        send(lambda: (src().at[rows(h)], dst().at[rows(1 - h)], flag(1 - h), left if h == 0 else right), is_away)

    def trade_g(i):
        for h in range(2):
            trade(lambda: g_hbm, lambda: g_work, lambda h: tg_sem.at[h, i], h, lambda h: chunk(h, i))

    def g_to_sibling(source, i, when):
        for h in range(2):
            send(lambda h=h: (source.at[chunk(h, i)], g_sib.at[chunk(h, i)], sg_sem.at[h, i], sibling), when)

    @pl.when(is_home)
    def _():
        for h in range(2):
            for i in range(2):
                load(g_hbm.at[chunk(h, i)], g_work.at[chunk(h, i)], tg_sem.at[h, i])
            load(q_hbm.at[whole(h)], q_work.at[whole(h)], tq_sem.at[h])

    prev_load.wait()

    @pl.loop(0, TOK // 16)
    def _(i):
        rows = pl.ds(pl.multiple_of(i * 16, 16), 16)
        values = x_buf[rows, :].astype(F32)
        scale = lax.rsqrt(jnp.mean(values * values, axis=-1, keepdims=True) + EPS)
        normed[away, rows, :] = (values * scale * gain_ref[...]).astype(BF16)

    def blocks_of(kind):
        xa = (x + kind) % 4
        return xa, (xa + 2) % 4

    sib_blocks = blocks_of(1 - away)

    def n_to_sibling(when):
        for j, block in enumerate(sib_blocks):

            def features(j=j, block=block):
                columns = pl.ds(pl.multiple_of(512 * block, 512), 512)
                return normed.at[0, :, columns], n_sib.at[:, pl.ds(512 * j, 512)], sn_sem.at[j], sibling

            send(features, when)

    for h in range(2):
        arrive(w_piece(0, 0, h), w_flag(0, 0, h))

    @pl.when(is_away)
    def _():
        spread_own(lambda h: w_piece(0, 0, h), is_away)
        for h in range(2):
            trade(lambda: normed.at[1], lambda: normed.at[0], lambda h: tn_sem.at[h], h)

    @pl.when(is_home)
    def _():
        own_across(half_rows, is_home)
        n_to_sibling(is_home)
        for i in range(2):
            g_to_sibling(g_hbm, i, is_home)

    x_load = load(x_hbm, x_buf, load_sem.at[0])

    def pass_on(k, when=None):
        for h in range(2):
            arrive(w_piece(k, -1, h), w_flag(k, -1, h))
            if h == 0:
                to_z(k, -1, 0, 1, when)
            arrive(w_piece(k, 1, h), w_flag(k, 1, h))
            if h == 1:
                to_z(k, 1, 1, -1, when)
        for h in range(2):
            to_sibling(k, -1, h, when)
            to_sibling(k, 1, h, when)

    @pl.when(is_home)
    def _():
        pass_on(0, is_home)

    for h in range(2):
        arrive(w_piece(1, 0, h), w_flag(1, 0, h))
        to_z(1, 0, h, 1)
        to_z(1, 0, h, -1)
        to_sibling(1, 0, h)

    @pl.when(is_away)
    def _():
        trade_g(0)
        pass_on(0, is_away)

    @pl.when(is_away)
    def _():
        trade_g(1)
        for h in range(2):
            arrive(normed.at[0, whole(h)], tn_sem.at[h])
        n_to_sibling(is_away)

    def pass_g(i):
        for h in range(2):
            arrive(g_work.at[chunk(h, i)], tg_sem.at[h, i])

        @pl.when(is_away)
        def _():
            g_to_sibling(g_work, i, is_away)

    pass_g(0)
    pass_on(1)
    pass_g(1)


    @pl.when(is_away)
    def _():
        for h in range(2):
            trade(lambda: q_hbm, lambda: q_work, lambda h: tq_sem.at[h], h)

    for j in range(2):
        arrive(n_sib.at[:, pl.ds(512 * j, 512)], sn_sem.at[j])
    for i in range(2):
        for h in range(2):
            arrive(g_sib.at[chunk(h, i)], sg_sem.at[h, i])
    xa, xb = blocks_of(away)

    def product(dz):
        to = (z + dz) % 4

        def columns(ref, block):
            return ref[:, pl.ds(pl.multiple_of(512 * block + OWN * to, OWN), OWN)]

        mine = jnp.concatenate([columns(normed.at[0], xa), columns(normed.at[0], xb)], axis=1)
        theirs = jnp.concatenate([columns(n_sib, 0), columns(n_sib, 1)], axis=1)

        @pl.loop(0, 4)
        def _(j):
            span = pl.ds(pl.multiple_of(j * 768, 768), 768)
            dims = (((0,), (0,)), ((), ()))
            total = lax.dot_general(mine, g_work[:, span], dims, preferred_element_type=F32)
            total += lax.dot_general(theirs, g_sib[:, span], dims, preferred_element_type=F32)
            dw[dz, :, span] = total.astype(BF16)

    def d_piece(dz, k, h):
        at_home = 128 * k + 64 * h
        at_away = 128 * k if h == 1 else 192 - 128 * k
        return dw.at[dz, pl.ds(pl.multiple_of(at_home + away * (at_away - at_home), PIECE), PIECE)]

    product(2)

    def farthest(k):
        return [
            send(lambda: (d_piece(2, k, 0), r1.at[0, k], r1_sem.at[k], up)),
            send(lambda: (d_piece(2, k, 1), r1.at[1, k], r1_sem.at[2 + k], down)),
        ]

    first, second = farthest(1), farthest(0)

    for k in range(2):
        for h in range(2):
            arrive(w_piece(k, 2, h), w_flag(k, 2, h))
            to_sibling(k, 2, h)

    product(1)
    product(3)

    def to_next(k, h, way):
        dz, side = (1, 0) if way == 1 else (3, 1)
        send(lambda: (d_piece(dz, k, h), r2.at[side, k, h], r2_sem.at[4 * side + 2 * k + h], up if way == 1 else down))

    def add_into(target, term):
        @pl.loop(0, QKV // 512)
        def _(j):
            span = pl.ds(pl.multiple_of(j * 512, 512), 512)
            target[:, span] = (target[:, span].astype(F32) + term[:, span].astype(F32)).astype(BF16)

    def direct(k):
        to_next(k, 1, 1)
        to_next(k, 0, -1)

    def summed(k):
        arrive(r1.at[0, k], r1_sem.at[k])
        add_into(d_piece(1, k, 0), r1.at[0, k])
        to_next(k, 0, 1)
        arrive(r1.at[1, k], r1_sem.at[2 + k])
        add_into(d_piece(3, k, 1), r1.at[1, k])
        to_next(k, 1, -1)

    for n in first:
        wait_sent(n)
    direct(1)
    product(0)

    def gain_copy(j, source):
        return pltpu.make_async_remote_copy(
            src_ref=gain_all.at[source], dst_ref=gain_all.at[source], send_sem=gsend_sem.at[j], recv_sem=gg_sem.at[source],
            device_id=(s, (f + j) % 16), device_id_type=MESH,
        )

    for dz in range(4):
        for k in range(2):
            for h in range(2):
                arrive(w_piece(k, dz, h, 1), ws_flag(k, dz, h))

    def gain_blocks(start, stop):
        @pl.loop(start, stop)
        def _(j):
            rows = pl.ds(pl.multiple_of(256 * j, 256), 256)
            out = lax.dot_general(g_work[...], w_full[rows, :], (((1,), (1,)), ((), ())), preferred_element_type=F32)
            gain_part[:, rows] = jnp.sum(out * normed[0, :, rows].astype(F32), axis=0, keepdims=True)

    gain_blocks(0, 8)

    slot = 4 * (x // 2) + z

    @pl.when(is_away)
    def _():
        send(lambda: (gain_part, gain_sib, gp_sem, sibling), is_away)

    @pl.when(is_home)
    def _():
        arrive(gain_sib, gp_sem)
        gain_all[slot, :, :] = gain_part[...] + gain_sib[...]

        @pl.loop(1, 16)
        def _(j):
            gain_copy(j, slot).start()

    for h in range(2):
        arrive(q_work.at[whole(h)], tq_sem.at[h])

    def direction(block):
        @pl.loop(0, 2)
        def _(j):
            rows = pl.ds(pl.multiple_of(512 * block + 256 * j, 256), 256)
            out = lax.dot_general(q_work[...], w_full[rows, :], (((1,), (1,)), ((), ())), preferred_element_type=F32)
            dirs[0, :, rows] = out.astype(BF16)

        @pl.when(is_away)
        def _():
            columns = pl.ds(512 * block, 512)
            for h in range(2):
                trade(lambda: dirs.at[0, :, columns], lambda: dirs.at[1, :, columns], lambda h: rd_sem.at[h, block], h)

    direction(0)
    direction(1)
    for n in second:
        wait_sent(n)
    summed(1)
    direct(0)
    direction(2)
    direction(3)
    summed(0)

    @pl.when(is_away)
    def _():
        for h in range(2):
            for block in range(4):
                arrive(dirs.at[1, whole(h), pl.ds(512 * block, 512)], rd_sem.at[h, block])

    x_load.wait()
    res_load.wait()
    for part in range(4):

        @pl.loop(0, 8)
        def _(i):
            rows = pl.ds(pl.multiple_of(128 * part + i * 16, 16), 16)
            values = x_buf[rows, :].astype(F32)
            scale = lax.rsqrt(jnp.mean(values * values, axis=-1, keepdims=True) + EPS)
            gained = gain_ref[...] * dirs[away, rows, :].astype(F32)
            inner = jnp.mean(gained * values, axis=-1, keepdims=True)
            out = res_buf[rows, :].astype(F32) + scale * gained - values * (scale * scale * scale * inner)
            res_buf[rows, :] = out.astype(BF16)

        @pl.when(has_before)
        def _():
            rows = pl.ds(128 * part, 128)
            send(lambda part=part: (res_buf.at[rows], up_hbm.at[rows], lg_sem.at[part], before), has_before)

    def sum_into(target, k, h):
        @pl.loop(0, QKV // 512)
        def _(j):
            span = pl.ds(pl.multiple_of(j * 512, 512), 512)
            total = target[:, span].astype(F32) + r2[0, k, h, :, span].astype(F32) + r2[1, k, h, :, span].astype(F32)
            target[:, span] = total.astype(BF16)

    def r2_arrive(k, h):
        arrive(r2.at[0, k, h], r2_sem.at[2 * k + h])
        arrive(r2.at[1, k, h], r2_sem.at[4 + 2 * k + h])

    def to_owner(k, h):
        send(lambda: (d_piece(0, k, h), r4.at[k, 1 - h], r4_sem.at[k, 1 - h], left if h == k else right), is_away)

    for h in range(2):
        r2_arrive(1, h)
        sum_into(d_piece(0, 1, h), 1, h)

        @pl.when(is_home)
        def _():
            send(lambda h=h: (d_piece(0, 1, h), r3.at[h], r3_sem.at[h], across), is_home)

        @pl.when(is_away)
        def _():
            to_owner(1, h)

    for h in range(2):
        r2_arrive(0, h)

        @pl.when(is_away)
        def _():
            sum_into(d_piece(0, 0, h), 0, h)
            to_owner(0, h)

        @pl.when(is_home)
        def _():
            arrive(r3.at[h], r3_sem.at[h])
            target = d_piece(0, 0, h)

            @pl.loop(0, QKV // 512)
            def _(j):
                span = pl.ds(pl.multiple_of(j * 512, 512), 512)
                total = target[:, span].astype(F32) + r2[0, 0, h, :, span].astype(F32) + r2[1, 0, h, :, span].astype(F32)
                wout[pl.ds(PIECE * h, PIECE), span] = total + r3[h, :, span].astype(F32)

    @pl.when(is_away)
    def _():
        for h in range(2):
            for k in range(2):
                arrive(r4.at[k, h], r4_sem.at[k, h])

            @pl.loop(0, QKV // 512)
            def _(j):
                span = pl.ds(pl.multiple_of(j * 512, 512), 512)
                wout[pl.ds(PIECE * h, PIECE), span] = r4[0, h, :, span].astype(F32) + r4[1, h, :, span].astype(F32)

    w_store = load(wout, wg_hbm, load_sem.at[3])

    for j in range(8):

        @pl.when(is_away | (slot != j))
        def _():
            arrive(gain_all.at[j], gg_sem.at[j])

    gg_ref[...] = jnp.sum(gain_all[...], axis=0) / gain_ref[...]

    @pl.when(s < 7)
    def _():
        for part in range(4):
            rows = pl.ds(128 * part, 128)
            arrive(up_hbm.at[rows], lg_sem.at[part])

    @pl.when(is_home)
    def _():
        @pl.loop(1, 16)
        def _(j):
            gain_copy(j, slot).wait_send()

    w_store.wait()
    for n in range(len(sent)):
        wait_sent(n)


SENDS = 140


def local(layer_input, resid_grad, qkv_grad, prev_input, prev_qkv_grad, qkv_weight, norm_gain):
    hbm = pl.BlockSpec(memory_space=pl.ANY)
    vmem = pl.BlockSpec(memory_space=pltpu.VMEM)
    dma = pltpu.SemaphoreType.DMA
    received, weight_grad, gain_grad = pl.pallas_call(
        kernel,
        out_shape=(
            jax.ShapeDtypeStruct((TOK, D), BF16),
            jax.ShapeDtypeStruct((OWN, QKV), F32),
            jax.ShapeDtypeStruct((1, D), F32),
        ),
        in_specs=[hbm] * 6 + [vmem],
        out_specs=(hbm, hbm, vmem),
        scratch_shapes=[
            pltpu.VMEM((D, QKV), BF16),
            pltpu.VMEM((4, 256, QKV), BF16),
            pltpu.VMEM((2, 2, PIECE, QKV), BF16),
            pltpu.VMEM((2, 2, 2, PIECE, QKV), BF16),
            pltpu.VMEM((2, PIECE, QKV), BF16),
            pltpu.VMEM((2, 2, PIECE, QKV), BF16),
            pltpu.VMEM((OWN, QKV), F32),
            pltpu.VMEM((TOK, QKV), BF16),
            pltpu.VMEM((2, TOK, D), BF16),
            pltpu.VMEM((TOK, D // 2), BF16),
            pltpu.VMEM((TOK, QKV), BF16),
            pltpu.VMEM((TOK, QKV), BF16),
            pltpu.VMEM((2, TOK, D), BF16),
            pltpu.VMEM((TOK, D), BF16),
            pltpu.VMEM((TOK, D), BF16),
            pltpu.VMEM((1, D), F32),
            pltpu.VMEM((1, D), F32),
            pltpu.VMEM((8, 1, D), F32),
            dma((4,)),
            dma((32,)),
            dma((32,)),
            dma((2,)),
            dma((2, 2)),
            dma((2,)),
            dma((2,)),
            dma((2, 2)),
            dma((2, 4)),
            dma((4,)),
            dma((8,)),
            dma((2,)),
            dma((2, 2)),
            dma((4,)),
            dma(()),
            dma((8,)),
            dma((SENDS,)),
            dma((16,)),
        ],
        compiler_params=pltpu.CompilerParams(collective_id=0, has_side_effects=True, vmem_limit_bytes=62 << 20),
    )(layer_input[0], resid_grad[0], qkv_grad[0], prev_input[0], prev_qkv_grad[0], qkv_weight[0], norm_gain)
    last = lax.axis_index("section") == lax.axis_size("section") - 1
    upstream_grad = jnp.where(last, jnp.zeros_like(received), received)
    return (upstream_grad[None], weight_grad[None], gain_grad)


def solution(mesh):
    tokens, whole = P("section", "fsdp", None), P("section", None)
    return jax.shard_map(
        local,
        mesh=mesh,
        in_specs=(tokens,) * 6 + (whole,),
        out_specs=(tokens, tokens, whole),
        check_vma=False,
    )
```

```python
import functools

import jax
import jax.numpy as jnp
from jax import lax
from jax.experimental import pallas as pl
from jax.experimental.pallas import tpu as pltpu
from jax.sharding import PartitionSpec as P

EPS = 1e-05
MESH = pl.DeviceIdType.MESH
TOK, D, QKV = 512, 2048, 3072
HALF = TOK // 2
CHUNK = HALF // 2
OWN = 128
PIECE = 64
F32, BF16 = jnp.float32, jnp.bfloat16


def kernel(
    x_hbm, res_hbm, q_hbm, prev_hbm, g_hbm, w_hbm, gain_ref,
    up_hbm, wg_hbm, gg_ref,
    w_full, dw, r1, r2, r3, r4, wout, q_work, normed, n_sib, g_work, g_sib, dirs, x_buf, res_buf, gain_part, gain_sib, gain_all,
    load_sem, w_sem, ws_sem, tn_sem, tg_sem, tq_sem, sn_sem, sg_sem, rd_sem, r1_sem, r2_sem, r3_sem, r4_sem, lg_sem, gp_sem, gg_sem,
    send_sem, gsend_sem,
):
    s, f = lax.axis_index("section"), lax.axis_index("fsdp")
    c, x, z = s % 2, f // 4, f % 4
    away = (c + x) % 2
    is_away, is_home, has_before = away == 1, away == 0, s > 0

    def at(section, x_to, z_to):
        return (section, ((x_to + 4) % 4) * 4 + (z_to + 4) % 4)

    sib_section = s + 1 - 2 * c
    sibling, across = at(sib_section, x, z), at(s, x + 2, z)
    up, down = at(s, x, z + 1), at(s, x, z - 1)
    left, right = at(sib_section, x - 1, z), at(sib_section, x + 1, z)
    before, after = ((s + 7) % 8, f), ((s + 1) % 8, f)

    sent = []

    def send(make, when=None):
        n = len(sent)

        def build():
            src, dst, recv, device = make()
            return pltpu.make_async_remote_copy(
                src_ref=src, dst_ref=dst, send_sem=send_sem.at[n], recv_sem=recv, device_id=device, device_id_type=MESH
            )

        sent.append([build, when])
        build().start()
        return n

    def wait_sent(n):
        build, when = sent[n]
        if build is None:
            return
        sent[n][0] = None
        if when is None:
            build().wait_send()
        else:
            pl.when(when)(lambda: build().wait_send())

    def load(src, dst, sem):
        copy = pltpu.make_async_copy(src, dst, sem)
        copy.start()
        return copy

    def arrive(dst, sem):
        pltpu.make_async_copy(dst, dst, sem).wait()

    barrier = pltpu.get_barrier_semaphore()

    def greet(device):
        pl.semaphore_signal(barrier, inc=1, device_id=device, device_id_type=MESH)

    @pl.loop(1, 16)
    def _(j):
        greet((s, (f + j) % 16))

    greet(sibling)

    @pl.when(is_away)
    def _():
        greet(left)
        greet(right)

    goes_down = (c == 0) & (s > 0)
    comes_down = (c == 1) & (s < 7)

    @pl.when(goes_down)
    def _():
        greet(before)

    @pl.when(comes_down)
    def _():
        greet(after)

    pl.semaphore_wait(barrier, 16 + 2 * away + (goes_down | comes_down).astype(jnp.int32))

    def w_piece(k, dz, h, flip=0):
        kind = away if flip == 0 else 1 - away
        xv = x + 2 * k
        owner = (xv + 3 * kind) % 4 if h == 0 else (xv + kind) % 4
        inner = PIECE * kind if h == 0 else PIECE * (1 - kind)
        start = (4 * owner + (z + dz + 4) % 4) * OWN + inner
        return w_full.at[pl.ds(pl.multiple_of(start, PIECE), PIECE)]

    def w_flag(k, dz, h):
        return w_sem.at[8 * ((dz + 4) % 4) + 2 * k + h]

    def ws_flag(k, dz, h):
        return ws_sem.at[8 * ((dz + 4) % 4) + 2 * k + h]

    def to_sibling(k, dz, h, when=None):
        send(lambda: (w_piece(k, dz, h), w_piece(k, dz, h), ws_flag(k, dz, h), sibling), when)

    def to_z(k, dz, h, way, when=None):
        send(lambda: (w_piece(k, dz, h), w_piece(k, dz, h), w_flag(k, dz - way, h), up if way == 1 else down), when)

    def own_across(source, when):
        for h in range(2):
            send(lambda h=h: (source(h), w_piece(0, 0, h), w_flag(1, 0, h), across), when)

    def spread_own(source, when):
        for h in range(2):
            send(lambda h=h: (source(h), w_piece(0, 0, h), w_flag(0, -1, h), up), when)
            send(lambda h=h: (source(h), w_piece(0, 0, h), w_flag(0, 1, h), down), when)
        for h in range(2):
            send(lambda h=h: (source(h), w_piece(0, 0, h), ws_flag(0, 0, h), sibling), when)

    def half_rows(h):
        return w_hbm.at[pl.ds(PIECE * h, PIECE)]

    @pl.when(is_home)
    def _():
        spread_own(half_rows, is_home)
        for h in range(2):
            load(half_rows(h), w_piece(0, 0, h), w_flag(0, 0, h))

    own_rows = pl.multiple_of(f * OWN, OWN)

    @pl.when(is_away)
    def _():
        for k in range(2):
            for h in range(2):

                def own_piece(k=k, h=h):
                    rows = w_full.at[pl.ds(pl.multiple_of(own_rows + PIECE * h, PIECE), PIECE)]
                    return half_rows(h), rows, w_flag(k, 0, 1 - h), right if h != k else left

                send(own_piece, is_away)

    prev_load = load(prev_hbm, x_buf, load_sem.at[0])
    res_load = load(res_hbm, res_buf, load_sem.at[2])

    def chunk(h, i):
        return pl.ds(HALF * h + CHUNK * i, CHUNK)

    def whole(h):
        return pl.ds(HALF * h, HALF)

    def trade(src, dst, flag, h, rows=whole):
        send(lambda: (src().at[rows(h)], dst().at[rows(1 - h)], flag(1 - h), left if h == 0 else right), is_away)

    def trade_g(i):
        for h in range(2):
            trade(lambda: g_hbm, lambda: g_work, lambda h: tg_sem.at[h, i], h, lambda h: chunk(h, i))

    def g_to_sibling(source, i, when):
        for h in range(2):
            send(lambda h=h: (source.at[chunk(h, i)], g_sib.at[chunk(h, i)], sg_sem.at[h, i], sibling), when)

    @pl.when(is_home)
    def _():
        for h in range(2):
            for i in range(2):
                load(g_hbm.at[chunk(h, i)], g_work.at[chunk(h, i)], tg_sem.at[h, i])
            load(q_hbm.at[whole(h)], q_work.at[whole(h)], tq_sem.at[h])

    prev_load.wait()

    @pl.loop(0, TOK // 16)
    def _(i):
        rows = pl.ds(pl.multiple_of(i * 16, 16), 16)
        values = x_buf[rows, :].astype(F32)
        scale = lax.rsqrt(jnp.mean(values * values, axis=-1, keepdims=True) + EPS)
        normed[away, rows, :] = (values * scale * gain_ref[...]).astype(BF16)

    def blocks_of(kind):
        xa = (x + kind) % 4
        return xa, (xa + 2) % 4

    sib_blocks = blocks_of(1 - away)

    def n_to_sibling(when):
        for j, block in enumerate(sib_blocks):

            def features(j=j, block=block):
                columns = pl.ds(pl.multiple_of(512 * block, 512), 512)
                return normed.at[0, :, columns], n_sib.at[:, pl.ds(512 * j, 512)], sn_sem.at[j], sibling

            send(features, when)

    for h in range(2):
        arrive(w_piece(0, 0, h), w_flag(0, 0, h))

    @pl.when(is_away)
    def _():
        spread_own(lambda h: w_piece(0, 0, h), is_away)
        for h in range(2):
            trade(lambda: normed.at[1], lambda: normed.at[0], lambda h: tn_sem.at[h], h)

    @pl.when(is_home)
    def _():
        own_across(half_rows, is_home)
        n_to_sibling(is_home)
        for i in range(2):
            g_to_sibling(g_hbm, i, is_home)

    x_load = load(x_hbm, x_buf, load_sem.at[0])

    def pass_on(k, when=None):
        for h in range(2):
            arrive(w_piece(k, -1, h), w_flag(k, -1, h))
            if h == 0:
                to_z(k, -1, 0, 1, when)
            arrive(w_piece(k, 1, h), w_flag(k, 1, h))
            if h == 1:
                to_z(k, 1, 1, -1, when)
        for h in range(2):
            to_sibling(k, -1, h, when)
            to_sibling(k, 1, h, when)

    @pl.when(is_home)
    def _():
        pass_on(0, is_home)

    for h in range(2):
        arrive(w_piece(1, 0, h), w_flag(1, 0, h))
        to_z(1, 0, h, 1)
        to_z(1, 0, h, -1)
        to_sibling(1, 0, h)

    @pl.when(is_away)
    def _():
        trade_g(0)
        pass_on(0, is_away)

    @pl.when(is_away)
    def _():
        trade_g(1)
        for h in range(2):
            arrive(normed.at[0, whole(h)], tn_sem.at[h])
        n_to_sibling(is_away)

    def pass_g(i):
        for h in range(2):
            arrive(g_work.at[chunk(h, i)], tg_sem.at[h, i])

        @pl.when(is_away)
        def _():
            g_to_sibling(g_work, i, is_away)

    pass_g(0)
    pass_on(1)
    pass_g(1)


    @pl.when(is_away)
    def _():
        for h in range(2):
            trade(lambda: q_hbm, lambda: q_work, lambda h: tq_sem.at[h], h)

    for j in range(2):
        arrive(n_sib.at[:, pl.ds(512 * j, 512)], sn_sem.at[j])
    for i in range(2):
        for h in range(2):
            arrive(g_sib.at[chunk(h, i)], sg_sem.at[h, i])
    xa, xb = blocks_of(away)

    def product(dz):
        to = (z + dz) % 4

        def columns(ref, block):
            return ref[:, pl.ds(pl.multiple_of(512 * block + OWN * to, OWN), OWN)]

        mine = jnp.concatenate([columns(normed.at[0], xa), columns(normed.at[0], xb)], axis=1)
        theirs = jnp.concatenate([columns(n_sib, 0), columns(n_sib, 1)], axis=1)

        @pl.loop(0, 4)
        def _(j):
            span = pl.ds(pl.multiple_of(j * 768, 768), 768)
            dims = (((0,), (0,)), ((), ()))
            total = lax.dot_general(mine, g_work[:, span], dims, preferred_element_type=F32)
            total += lax.dot_general(theirs, g_sib[:, span], dims, preferred_element_type=F32)
            dw[dz, :, span] = total.astype(BF16)

    def d_piece(dz, k, h):
        at_home = 128 * k + 64 * h
        at_away = 128 * k if h == 1 else 192 - 128 * k
        return dw.at[dz, pl.ds(pl.multiple_of(at_home + away * (at_away - at_home), PIECE), PIECE)]

    product(2)

    def farthest(k):
        return [
            send(lambda: (d_piece(2, k, 0), r1.at[0, k], r1_sem.at[k], up)),
            send(lambda: (d_piece(2, k, 1), r1.at[1, k], r1_sem.at[2 + k], down)),
        ]

    first, second = farthest(1), farthest(0)

    for k in range(2):
        for h in range(2):
            arrive(w_piece(k, 2, h), w_flag(k, 2, h))
            to_sibling(k, 2, h)

    product(1)
    product(3)

    def to_next(k, h, way):
        dz, side = (1, 0) if way == 1 else (3, 1)
        send(lambda: (d_piece(dz, k, h), r2.at[side, k, h], r2_sem.at[4 * side + 2 * k + h], up if way == 1 else down))

    def add_into(target, term):
        @pl.loop(0, QKV // 512)
        def _(j):
            span = pl.ds(pl.multiple_of(j * 512, 512), 512)
            target[:, span] = (target[:, span].astype(F32) + term[:, span].astype(F32)).astype(BF16)

    def direct(k):
        to_next(k, 1, 1)
        to_next(k, 0, -1)

    def summed(k):
        arrive(r1.at[0, k], r1_sem.at[k])
        add_into(d_piece(1, k, 0), r1.at[0, k])
        to_next(k, 0, 1)
        arrive(r1.at[1, k], r1_sem.at[2 + k])
        add_into(d_piece(3, k, 1), r1.at[1, k])
        to_next(k, 1, -1)

    product(0)
    for dz in range(4):
        for k in range(2):
            for h in range(2):
                arrive(w_piece(k, dz, h, 1), ws_flag(k, dz, h))

    def gain_blocks(start, stop):
        @pl.loop(start, stop)
        def _(j):
            rows = pl.ds(pl.multiple_of(256 * j, 256), 256)
            out = lax.dot_general(g_work[...], w_full[rows, :], (((1,), (1,)), ((), ())), preferred_element_type=F32)
            gain_part[:, rows] = jnp.sum(out * normed[0, :, rows].astype(F32), axis=0, keepdims=True)

    gain_blocks(0, 4)

    for n in first:
        wait_sent(n)
    direct(1)

    def gain_copy(j, source):
        return pltpu.make_async_remote_copy(
            src_ref=gain_all.at[source], dst_ref=gain_all.at[source], send_sem=gsend_sem.at[j], recv_sem=gg_sem.at[source],
            device_id=(s, (f + j) % 16), device_id_type=MESH,
        )


    for h in range(2):
        arrive(q_work.at[whole(h)], tq_sem.at[h])

    def direction(block):
        @pl.loop(0, 2)
        def _(j):
            rows = pl.ds(pl.multiple_of(512 * block + 256 * j, 256), 256)
            out = lax.dot_general(q_work[...], w_full[rows, :], (((1,), (1,)), ((), ())), preferred_element_type=F32)
            dirs[0, :, rows] = out.astype(BF16)

        @pl.when(is_away)
        def _():
            columns = pl.ds(512 * block, 512)
            for h in range(2):
                trade(lambda: dirs.at[0, :, columns], lambda: dirs.at[1, :, columns], lambda h: rd_sem.at[h, block], h)

    direction(0)
    direction(1)
    for n in second:
        wait_sent(n)
    summed(1)
    direct(0)
    direction(2)
    direction(3)
    summed(0)
    gain_blocks(4, 8)

    @pl.when(is_away)
    def _():
        for h in range(2):
            for block in range(4):
                arrive(dirs.at[1, whole(h), pl.ds(512 * block, 512)], rd_sem.at[h, block])

    x_load.wait()
    res_load.wait()
    for part in range(4):

        @pl.loop(0, 8)
        def _(i):
            rows = pl.ds(pl.multiple_of(128 * part + i * 16, 16), 16)
            values = x_buf[rows, :].astype(F32)
            scale = lax.rsqrt(jnp.mean(values * values, axis=-1, keepdims=True) + EPS)
            gained = gain_ref[...] * dirs[away, rows, :].astype(F32)
            inner = jnp.mean(gained * values, axis=-1, keepdims=True)
            out = res_buf[rows, :].astype(F32) + scale * gained - values * (scale * scale * scale * inner)
            res_buf[rows, :] = out.astype(BF16)

        @pl.when(has_before)
        def _():
            rows = pl.ds(128 * part, 128)
            send(lambda part=part: (res_buf.at[rows], up_hbm.at[rows], lg_sem.at[part], before), has_before)

    slot = 4 * (x // 2) + z

    @pl.when(is_away)
    def _():
        send(lambda: (gain_part, gain_sib, gp_sem, sibling), is_away)

    @pl.when(is_home)
    def _():
        arrive(gain_sib, gp_sem)
        gain_all[slot, :, :] = gain_part[...] + gain_sib[...]

        @pl.loop(1, 16)
        def _(j):
            gain_copy(j, slot).start()

    def sum_into(target, k, h):
        @pl.loop(0, QKV // 512)
        def _(j):
            span = pl.ds(pl.multiple_of(j * 512, 512), 512)
            total = target[:, span].astype(F32) + r2[0, k, h, :, span].astype(F32) + r2[1, k, h, :, span].astype(F32)
            target[:, span] = total.astype(BF16)

    def r2_arrive(k, h):
        arrive(r2.at[0, k, h], r2_sem.at[2 * k + h])
        arrive(r2.at[1, k, h], r2_sem.at[4 + 2 * k + h])

    def to_owner(k, h):
        send(lambda: (d_piece(0, k, h), r4.at[k, 1 - h], r4_sem.at[k, 1 - h], left if h == k else right), is_away)

    for h in range(2):
        r2_arrive(1, h)
        sum_into(d_piece(0, 1, h), 1, h)

        @pl.when(is_home)
        def _():
            send(lambda h=h: (d_piece(0, 1, h), r3.at[h], r3_sem.at[h], across), is_home)

        @pl.when(is_away)
        def _():
            to_owner(1, h)

    for h in range(2):
        r2_arrive(0, h)

        @pl.when(is_away)
        def _():
            sum_into(d_piece(0, 0, h), 0, h)
            to_owner(0, h)

        @pl.when(is_home)
        def _():
            arrive(r3.at[h], r3_sem.at[h])
            target = d_piece(0, 0, h)

            @pl.loop(0, QKV // 512)
            def _(j):
                span = pl.ds(pl.multiple_of(j * 512, 512), 512)
                total = target[:, span].astype(F32) + r2[0, 0, h, :, span].astype(F32) + r2[1, 0, h, :, span].astype(F32)
                wout[pl.ds(PIECE * h, PIECE), span] = total + r3[h, :, span].astype(F32)

    @pl.when(is_away)
    def _():
        for h in range(2):
            for k in range(2):
                arrive(r4.at[k, h], r4_sem.at[k, h])

            @pl.loop(0, QKV // 512)
            def _(j):
                span = pl.ds(pl.multiple_of(j * 512, 512), 512)
                wout[pl.ds(PIECE * h, PIECE), span] = r4[0, h, :, span].astype(F32) + r4[1, h, :, span].astype(F32)

    w_store = load(wout, wg_hbm, load_sem.at[3])

    for j in range(8):

        @pl.when(is_away | (slot != j))
        def _():
            arrive(gain_all.at[j], gg_sem.at[j])

    gg_ref[...] = jnp.sum(gain_all[...], axis=0) / gain_ref[...]

    @pl.when(s < 7)
    def _():
        for part in range(4):
            rows = pl.ds(128 * part, 128)
            arrive(up_hbm.at[rows], lg_sem.at[part])

    @pl.when(is_home)
    def _():
        @pl.loop(1, 16)
        def _(j):
            gain_copy(j, slot).wait_send()

    w_store.wait()
    for n in range(len(sent)):
        wait_sent(n)


SENDS = 140


def place(received, weight, gain, up_out, weight_out, gain_out, up_buf, weight_buf, gain_buf, in_sem, out_sem):
    last = lax.axis_index("section") == 7
    parts = [(received, up_buf, up_out, pl.ds(128 * i, 128)) for i in range(4)]
    parts += [(weight, weight_buf, weight_out, pl.ds(32 * i, 32)) for i in range(4)]
    parts.append((gain, gain_buf, gain_out, pl.ds(0, 1)))
    reads = [pltpu.make_async_copy(src.at[rows], buf.at[rows], in_sem.at[i]) for i, (src, buf, _, rows) in enumerate(parts)]
    writes = [pltpu.make_async_copy(buf.at[rows], dst.at[rows], out_sem.at[i]) for i, (_, buf, dst, rows) in enumerate(parts)]
    for read in reads:
        read.start()
    for i in range(9):
        reads[i].wait()
        if i < 4:

            @pl.when(last)
            def _():
                up_buf[parts[i][3], :] = jnp.zeros((128, D), BF16)

        writes[i].start()
    for write in writes:
        write.wait()


def local(layer_input, resid_grad, qkv_grad, prev_input, prev_qkv_grad, qkv_weight, norm_gain):
    hbm = pl.BlockSpec(memory_space=pl.ANY)
    vmem = pl.BlockSpec(memory_space=pltpu.VMEM)
    dma = pltpu.SemaphoreType.DMA
    received, weight_grad, gain_grad = pl.pallas_call(
        kernel,
        out_shape=(
            jax.ShapeDtypeStruct((TOK, D), BF16),
            jax.ShapeDtypeStruct((OWN, QKV), F32),
            jax.ShapeDtypeStruct((1, D), F32),
        ),
        in_specs=[hbm] * 6 + [vmem],
        out_specs=(hbm, hbm, vmem),
        scratch_shapes=[
            pltpu.VMEM((D, QKV), BF16),
            pltpu.VMEM((4, 256, QKV), BF16),
            pltpu.VMEM((2, 2, PIECE, QKV), BF16),
            pltpu.VMEM((2, 2, 2, PIECE, QKV), BF16),
            pltpu.VMEM((2, PIECE, QKV), BF16),
            pltpu.VMEM((2, 2, PIECE, QKV), BF16),
            pltpu.VMEM((OWN, QKV), F32),
            pltpu.VMEM((TOK, QKV), BF16),
            pltpu.VMEM((2, TOK, D), BF16),
            pltpu.VMEM((TOK, D // 2), BF16),
            pltpu.VMEM((TOK, QKV), BF16),
            pltpu.VMEM((TOK, QKV), BF16),
            pltpu.VMEM((2, TOK, D), BF16),
            pltpu.VMEM((TOK, D), BF16),
            pltpu.VMEM((TOK, D), BF16),
            pltpu.VMEM((1, D), F32),
            pltpu.VMEM((1, D), F32),
            pltpu.VMEM((8, 1, D), F32),
            dma((4,)),
            dma((32,)),
            dma((32,)),
            dma((2,)),
            dma((2, 2)),
            dma((2,)),
            dma((2,)),
            dma((2, 2)),
            dma((2, 4)),
            dma((4,)),
            dma((8,)),
            dma((2,)),
            dma((2, 2)),
            dma((4,)),
            dma(()),
            dma((8,)),
            dma((SENDS,)),
            dma((16,)),
        ],
        compiler_params=pltpu.CompilerParams(collective_id=0, has_side_effects=True, vmem_limit_bytes=62 << 20),
    )(layer_input[0], resid_grad[0], qkv_grad[0], prev_input[0], prev_qkv_grad[0], qkv_weight[0], norm_gain)
    upstream_grad, weight_grad, gain_grad = pl.pallas_call(
        place,
        out_shape=(
            jax.ShapeDtypeStruct((TOK, D), BF16),
            jax.ShapeDtypeStruct((OWN, QKV), F32),
            jax.ShapeDtypeStruct((1, D), F32),
        ),
        in_specs=[hbm] * 3,
        out_specs=(hbm, hbm, hbm),
        scratch_shapes=[pltpu.VMEM((TOK, D), BF16), pltpu.VMEM((OWN, QKV), F32), pltpu.VMEM((1, D), F32), dma((9,)), dma((9,))],
    )(received, weight_grad, gain_grad)
    return (upstream_grad[None], weight_grad[None], gain_grad)


def solution(mesh):
    tokens, whole = P("section", "fsdp", None), P("section", None)
    return jax.shard_map(
        local,
        mesh=mesh,
        in_specs=(tokens,) * 6 + (whole,),
        out_specs=(tokens, tokens, whole),
        check_vma=False,
    )
```

```python
import functools

import jax
import jax.numpy as jnp
from jax import lax
from jax.experimental import pallas as pl
from jax.experimental.pallas import tpu as pltpu
from jax.sharding import PartitionSpec as P

EPS = 1e-05
MESH = pl.DeviceIdType.MESH
TOK, D, QKV = 512, 2048, 3072
HALF = TOK // 2
CHUNK = HALF // 2
OWN = 128
PIECE = 64
F32, BF16 = jnp.float32, jnp.bfloat16


def kernel(
    x_hbm, res_hbm, q_hbm, prev_hbm, g_hbm, w_hbm, gain_ref,
    up_hbm, wg_hbm, gg_ref,
    w_full, dw, r1, r2, r3, r4, wout, q_work, normed, n_sib, g_work, g_sib, dirs, x_buf, res_buf, gain_part, gain_sib, gain_all,
    load_sem, w_sem, ws_sem, tn_sem, tg_sem, tq_sem, sn_sem, sg_sem, rd_sem, r1_sem, r2_sem, r3_sem, r4_sem, lg_sem, gp_sem, gg_sem,
    send_sem, gsend_sem,
):
    s, f = lax.axis_index("section"), lax.axis_index("fsdp")
    c, x, z = s % 2, f // 4, f % 4
    away = (c + x) % 2
    is_away, is_home, has_before = away == 1, away == 0, s > 0

    def at(section, x_to, z_to):
        return (section, ((x_to + 4) % 4) * 4 + (z_to + 4) % 4)

    sib_section = s + 1 - 2 * c
    sibling, across = at(sib_section, x, z), at(s, x + 2, z)
    up, down = at(s, x, z + 1), at(s, x, z - 1)
    left, right = at(sib_section, x - 1, z), at(sib_section, x + 1, z)
    before, after = ((s + 7) % 8, f), ((s + 1) % 8, f)

    sent = []

    def send(make, when=None):
        n = len(sent)

        def build():
            src, dst, recv, device = make()
            return pltpu.make_async_remote_copy(
                src_ref=src, dst_ref=dst, send_sem=send_sem.at[n], recv_sem=recv, device_id=device, device_id_type=MESH
            )

        sent.append([build, when])
        build().start()
        return n

    def wait_sent(n):
        build, when = sent[n]
        if build is None:
            return
        sent[n][0] = None
        if when is None:
            build().wait_send()
        else:
            pl.when(when)(lambda: build().wait_send())

    def load(src, dst, sem):
        copy = pltpu.make_async_copy(src, dst, sem)
        copy.start()
        return copy

    def arrive(dst, sem):
        pltpu.make_async_copy(dst, dst, sem).wait()

    barrier = pltpu.get_barrier_semaphore()

    def greet(device):
        pl.semaphore_signal(barrier, inc=1, device_id=device, device_id_type=MESH)

    @pl.loop(1, 16)
    def _(j):
        greet((s, (f + j) % 16))

    greet(sibling)

    @pl.when(is_away)
    def _():
        greet(left)
        greet(right)

    goes_down = (c == 0) & (s > 0)
    comes_down = (c == 1) & (s < 7)

    @pl.when(goes_down)
    def _():
        greet(before)

    @pl.when(comes_down)
    def _():
        greet(after)

    pl.semaphore_wait(barrier, 16 + 2 * away + (goes_down | comes_down).astype(jnp.int32))

    def w_piece(k, dz, h, flip=0):
        kind = away if flip == 0 else 1 - away
        xv = x + 2 * k
        owner = (xv + 3 * kind) % 4 if h == 0 else (xv + kind) % 4
        inner = PIECE * kind if h == 0 else PIECE * (1 - kind)
        start = (4 * owner + (z + dz + 4) % 4) * OWN + inner
        return w_full.at[pl.ds(pl.multiple_of(start, PIECE), PIECE)]

    def w_flag(k, dz, h):
        return w_sem.at[8 * ((dz + 4) % 4) + 2 * k + h]

    def ws_flag(k, dz, h):
        return ws_sem.at[8 * ((dz + 4) % 4) + 2 * k + h]

    def to_sibling(k, dz, h, when=None):
        send(lambda: (w_piece(k, dz, h), w_piece(k, dz, h), ws_flag(k, dz, h), sibling), when)

    def to_z(k, dz, h, way, when=None):
        send(lambda: (w_piece(k, dz, h), w_piece(k, dz, h), w_flag(k, dz - way, h), up if way == 1 else down), when)

    def own_across(source, when):
        for h in range(2):
            send(lambda h=h: (source(h), w_piece(0, 0, h), w_flag(1, 0, h), across), when)

    def spread_own(source, when):
        for h in range(2):
            send(lambda h=h: (source(h), w_piece(0, 0, h), w_flag(0, -1, h), up), when)
            send(lambda h=h: (source(h), w_piece(0, 0, h), w_flag(0, 1, h), down), when)
        for h in range(2):
            send(lambda h=h: (source(h), w_piece(0, 0, h), ws_flag(0, 0, h), sibling), when)

    def half_rows(h):
        return w_hbm.at[pl.ds(PIECE * h, PIECE)]

    @pl.when(is_home)
    def _():
        spread_own(half_rows, is_home)
        for h in range(2):
            load(half_rows(h), w_piece(0, 0, h), w_flag(0, 0, h))

    own_rows = pl.multiple_of(f * OWN, OWN)

    @pl.when(is_away)
    def _():
        for k in range(2):
            for h in range(2):

                def own_piece(k=k, h=h):
                    rows = w_full.at[pl.ds(pl.multiple_of(own_rows + PIECE * h, PIECE), PIECE)]
                    return half_rows(h), rows, w_flag(k, 0, 1 - h), right if h != k else left

                send(own_piece, is_away)

    prev_load = load(prev_hbm, x_buf, load_sem.at[0])
    res_load = load(res_hbm, res_buf, load_sem.at[2])

    def chunk(h, i):
        return pl.ds(HALF * h + CHUNK * i, CHUNK)

    def whole(h):
        return pl.ds(HALF * h, HALF)

    def trade(src, dst, flag, h, rows=whole):
        send(lambda: (src().at[rows(h)], dst().at[rows(1 - h)], flag(1 - h), left if h == 0 else right), is_away)

    def trade_g(i):
        for h in range(2):
            trade(lambda: g_hbm, lambda: g_work, lambda h: tg_sem.at[h, i], h, lambda h: chunk(h, i))

    def g_to_sibling(source, i, when):
        for h in range(2):
            send(lambda h=h: (source.at[chunk(h, i)], g_sib.at[chunk(h, i)], sg_sem.at[h, i], sibling), when)

    @pl.when(is_home)
    def _():
        for h in range(2):
            for i in range(2):
                load(g_hbm.at[chunk(h, i)], g_work.at[chunk(h, i)], tg_sem.at[h, i])
            load(q_hbm.at[whole(h)], q_work.at[whole(h)], tq_sem.at[h])

    prev_load.wait()

    @pl.loop(0, TOK // 16)
    def _(i):
        rows = pl.ds(pl.multiple_of(i * 16, 16), 16)
        values = x_buf[rows, :].astype(F32)
        scale = lax.rsqrt(jnp.mean(values * values, axis=-1, keepdims=True) + EPS)
        normed[away, rows, :] = (values * scale * gain_ref[...]).astype(BF16)

    def blocks_of(kind):
        xa = (x + kind) % 4
        return xa, (xa + 2) % 4

    sib_blocks = blocks_of(1 - away)

    def n_to_sibling(when):
        for j, block in enumerate(sib_blocks):

            def features(j=j, block=block):
                columns = pl.ds(pl.multiple_of(512 * block, 512), 512)
                return normed.at[0, :, columns], n_sib.at[:, pl.ds(512 * j, 512)], sn_sem.at[j], sibling

            send(features, when)

    for h in range(2):
        arrive(w_piece(0, 0, h), w_flag(0, 0, h))

    @pl.when(is_away)
    def _():
        spread_own(lambda h: w_piece(0, 0, h), is_away)
        for h in range(2):
            trade(lambda: normed.at[1], lambda: normed.at[0], lambda h: tn_sem.at[h], h)
        trade_g(0)

    @pl.when(is_home)
    def _():
        own_across(half_rows, is_home)
        n_to_sibling(is_home)
        for i in range(2):
            g_to_sibling(g_hbm, i, is_home)

    x_load = load(x_hbm, x_buf, load_sem.at[0])

    def pass_on(k, when=None):
        for h in range(2):
            arrive(w_piece(k, -1, h), w_flag(k, -1, h))
            if h == 0:
                to_z(k, -1, 0, 1, when)
            arrive(w_piece(k, 1, h), w_flag(k, 1, h))
            if h == 1:
                to_z(k, 1, 1, -1, when)
        for h in range(2):
            to_sibling(k, -1, h, when)
            to_sibling(k, 1, h, when)

    @pl.when(is_home)
    def _():
        pass_on(0, is_home)

    for h in range(2):
        arrive(w_piece(1, 0, h), w_flag(1, 0, h))
        to_z(1, 0, h, 1)
        to_z(1, 0, h, -1)
        to_sibling(1, 0, h)

    @pl.when(is_away)
    def _():
        pass_on(0, is_away)

    @pl.when(is_away)
    def _():
        trade_g(1)
        for h in range(2):
            arrive(normed.at[0, whole(h)], tn_sem.at[h])
        n_to_sibling(is_away)

    def pass_g(i):
        for h in range(2):
            arrive(g_work.at[chunk(h, i)], tg_sem.at[h, i])

        @pl.when(is_away)
        def _():
            g_to_sibling(g_work, i, is_away)

    pass_g(0)
    pass_on(1)
    pass_g(1)


    @pl.when(is_away)
    def _():
        for h in range(2):
            trade(lambda: q_hbm, lambda: q_work, lambda h: tq_sem.at[h], h)

    for j in range(2):
        arrive(n_sib.at[:, pl.ds(512 * j, 512)], sn_sem.at[j])
    for i in range(2):
        for h in range(2):
            arrive(g_sib.at[chunk(h, i)], sg_sem.at[h, i])
    xa, xb = blocks_of(away)

    def product(dz):
        to = (z + dz) % 4

        def columns(ref, block):
            return ref[:, pl.ds(pl.multiple_of(512 * block + OWN * to, OWN), OWN)]

        mine = jnp.concatenate([columns(normed.at[0], xa), columns(normed.at[0], xb)], axis=1)
        theirs = jnp.concatenate([columns(n_sib, 0), columns(n_sib, 1)], axis=1)

        @pl.loop(0, 4)
        def _(j):
            span = pl.ds(pl.multiple_of(j * 768, 768), 768)
            dims = (((0,), (0,)), ((), ()))
            total = lax.dot_general(mine, g_work[:, span], dims, preferred_element_type=F32)
            total += lax.dot_general(theirs, g_sib[:, span], dims, preferred_element_type=F32)
            dw[dz, :, span] = total.astype(BF16)

    def d_piece(dz, k, h):
        at_home = 128 * k + 64 * h
        at_away = 128 * k if h == 1 else 192 - 128 * k
        return dw.at[dz, pl.ds(pl.multiple_of(at_home + away * (at_away - at_home), PIECE), PIECE)]

    product(2)

    def farthest(k):
        return [
            send(lambda: (d_piece(2, k, 0), r1.at[0, k], r1_sem.at[k], up)),
            send(lambda: (d_piece(2, k, 1), r1.at[1, k], r1_sem.at[2 + k], down)),
        ]

    first, second = farthest(1), farthest(0)

    for k in range(2):
        for h in range(2):
            arrive(w_piece(k, 2, h), w_flag(k, 2, h))
            to_sibling(k, 2, h)

    product(1)
    product(3)

    def to_next(k, h, way):
        dz, side = (1, 0) if way == 1 else (3, 1)
        send(lambda: (d_piece(dz, k, h), r2.at[side, k, h], r2_sem.at[4 * side + 2 * k + h], up if way == 1 else down))

    def add_into(target, term):
        @pl.loop(0, QKV // 512)
        def _(j):
            span = pl.ds(pl.multiple_of(j * 512, 512), 512)
            target[:, span] = (target[:, span].astype(F32) + term[:, span].astype(F32)).astype(BF16)

    def direct(k):
        to_next(k, 1, 1)
        to_next(k, 0, -1)

    def summed(k):
        arrive(r1.at[0, k], r1_sem.at[k])
        add_into(d_piece(1, k, 0), r1.at[0, k])
        to_next(k, 0, 1)
        arrive(r1.at[1, k], r1_sem.at[2 + k])
        add_into(d_piece(3, k, 1), r1.at[1, k])
        to_next(k, 1, -1)

    product(0)
    for dz in range(4):
        for k in range(2):
            for h in range(2):
                arrive(w_piece(k, dz, h, 1), ws_flag(k, dz, h))

    def gain_blocks(start, stop):
        @pl.loop(start, stop)
        def _(j):
            rows = pl.ds(pl.multiple_of(256 * j, 256), 256)
            out = lax.dot_general(g_work[...], w_full[rows, :], (((1,), (1,)), ((), ())), preferred_element_type=F32)
            gain_part[:, rows] = jnp.sum(out * normed[0, :, rows].astype(F32), axis=0, keepdims=True)

    gain_blocks(0, 4)

    direct(1)

    def gain_copy(j, source):
        return pltpu.make_async_remote_copy(
            src_ref=gain_all.at[source], dst_ref=gain_all.at[source], send_sem=gsend_sem.at[j], recv_sem=gg_sem.at[source],
            device_id=(s, (f + j) % 16), device_id_type=MESH,
        )


    for h in range(2):
        arrive(q_work.at[whole(h)], tq_sem.at[h])

    def direction(block):
        @pl.loop(0, 2)
        def _(j):
            rows = pl.ds(pl.multiple_of(512 * block + 256 * j, 256), 256)
            out = lax.dot_general(q_work[...], w_full[rows, :], (((1,), (1,)), ((), ())), preferred_element_type=F32)
            dirs[0, :, rows] = out.astype(BF16)

        @pl.when(is_away)
        def _():
            columns = pl.ds(512 * block, 512)
            for h in range(2):
                trade(lambda: dirs.at[0, :, columns], lambda: dirs.at[1, :, columns], lambda h: rd_sem.at[h, block], h)

    direction(0)
    direction(1)
    for n in second:
        wait_sent(n)
    summed(1)
    direct(0)
    direction(2)
    direction(3)
    summed(0)

    @pl.when(is_away)
    def _():
        for h in range(2):
            for block in range(4):
                arrive(dirs.at[1, whole(h), pl.ds(512 * block, 512)], rd_sem.at[h, block])

    x_load.wait()
    res_load.wait()
    for part in range(4):

        @pl.loop(0, 8)
        def _(i):
            rows = pl.ds(pl.multiple_of(128 * part + i * 16, 16), 16)
            values = x_buf[rows, :].astype(F32)
            scale = lax.rsqrt(jnp.mean(values * values, axis=-1, keepdims=True) + EPS)
            gained = gain_ref[...] * dirs[away, rows, :].astype(F32)
            inner = jnp.mean(gained * values, axis=-1, keepdims=True)
            out = res_buf[rows, :].astype(F32) + scale * gained - values * (scale * scale * scale * inner)
            res_buf[rows, :] = out.astype(BF16)

        @pl.when(has_before)
        def _():
            rows = pl.ds(128 * part, 128)
            send(lambda part=part: (res_buf.at[rows], up_hbm.at[rows], lg_sem.at[part], before), has_before)

    def sum_into(target, k, h):
        @pl.loop(0, QKV // 512)
        def _(j):
            span = pl.ds(pl.multiple_of(j * 512, 512), 512)
            total = target[:, span].astype(F32) + r2[0, k, h, :, span].astype(F32) + r2[1, k, h, :, span].astype(F32)
            target[:, span] = total.astype(BF16)

    def r2_arrive(k, h):
        arrive(r2.at[0, k, h], r2_sem.at[2 * k + h])
        arrive(r2.at[1, k, h], r2_sem.at[4 + 2 * k + h])

    def to_owner(k, h):
        send(lambda: (d_piece(0, k, h), r4.at[k, 1 - h], r4_sem.at[k, 1 - h], left if h == k else right), is_away)

    for h in range(2):
        r2_arrive(1, h)
        sum_into(d_piece(0, 1, h), 1, h)

        @pl.when(is_home)
        def _():
            send(lambda h=h: (d_piece(0, 1, h), r3.at[h], r3_sem.at[h], across), is_home)

        @pl.when(is_away)
        def _():
            to_owner(1, h)

    gain_blocks(4, 8)

    slot = 4 * (x // 2) + z

    @pl.when(is_away)
    def _():
        send(lambda: (gain_part, gain_sib, gp_sem, sibling), is_away)

    @pl.when(is_home)
    def _():
        arrive(gain_sib, gp_sem)
        gain_all[slot, :, :] = gain_part[...] + gain_sib[...]

        @pl.loop(1, 16)
        def _(j):
            gain_copy(j, slot).start()

    for h in range(2):
        r2_arrive(0, h)

        @pl.when(is_away)
        def _():
            sum_into(d_piece(0, 0, h), 0, h)
            to_owner(0, h)

        @pl.when(is_home)
        def _():
            arrive(r3.at[h], r3_sem.at[h])
            target = d_piece(0, 0, h)

            @pl.loop(0, QKV // 512)
            def _(j):
                span = pl.ds(pl.multiple_of(j * 512, 512), 512)
                total = target[:, span].astype(F32) + r2[0, 0, h, :, span].astype(F32) + r2[1, 0, h, :, span].astype(F32)
                wout[pl.ds(PIECE * h, PIECE), span] = total + r3[h, :, span].astype(F32)

    @pl.when(is_away)
    def _():
        for h in range(2):
            for k in range(2):
                arrive(r4.at[k, h], r4_sem.at[k, h])

            @pl.loop(0, QKV // 512)
            def _(j):
                span = pl.ds(pl.multiple_of(j * 512, 512), 512)
                wout[pl.ds(PIECE * h, PIECE), span] = r4[0, h, :, span].astype(F32) + r4[1, h, :, span].astype(F32)

    w_store = load(wout, wg_hbm, load_sem.at[3])

    for j in range(8):

        @pl.when(is_away | (slot != j))
        def _():
            arrive(gain_all.at[j], gg_sem.at[j])

    gg_ref[...] = jnp.sum(gain_all[...], axis=0) / gain_ref[...]

    @pl.when(s < 7)
    def _():
        for part in range(4):
            rows = pl.ds(128 * part, 128)
            arrive(up_hbm.at[rows], lg_sem.at[part])

    @pl.when(is_home)
    def _():
        @pl.loop(1, 16)
        def _(j):
            gain_copy(j, slot).wait_send()

    w_store.wait()
    for n in range(len(sent)):
        wait_sent(n)


SENDS = 140


def place(received, weight, gain, up_out, weight_out, gain_out, up_buf, weight_buf, gain_buf, in_sem, out_sem):
    last = lax.axis_index("section") == 7
    parts = [(received, up_buf, up_out, pl.ds(128 * i, 128)) for i in range(4)]
    parts += [(weight, weight_buf, weight_out, pl.ds(32 * i, 32)) for i in range(4)]
    parts.append((gain, gain_buf, gain_out, pl.ds(0, 1)))
    reads = [pltpu.make_async_copy(src.at[rows], buf.at[rows], in_sem.at[i]) for i, (src, buf, _, rows) in enumerate(parts)]
    writes = [pltpu.make_async_copy(buf.at[rows], dst.at[rows], out_sem.at[i]) for i, (_, buf, dst, rows) in enumerate(parts)]
    for read in reads:
        read.start()
    for i in range(9):
        reads[i].wait()
        if i < 4:

            @pl.when(last)
            def _():
                up_buf[parts[i][3], :] = jnp.zeros((128, D), BF16)

        writes[i].start()
    for write in writes:
        write.wait()


def local(layer_input, resid_grad, qkv_grad, prev_input, prev_qkv_grad, qkv_weight, norm_gain):
    hbm = pl.BlockSpec(memory_space=pl.ANY)
    vmem = pl.BlockSpec(memory_space=pltpu.VMEM)
    dma = pltpu.SemaphoreType.DMA
    received, weight_grad, gain_grad = pl.pallas_call(
        kernel,
        out_shape=(
            jax.ShapeDtypeStruct((TOK, D), BF16),
            jax.ShapeDtypeStruct((OWN, QKV), F32),
            jax.ShapeDtypeStruct((1, D), F32),
        ),
        in_specs=[hbm] * 6 + [vmem],
        out_specs=(hbm, hbm, vmem),
        scratch_shapes=[
            pltpu.VMEM((D, QKV), BF16),
            pltpu.VMEM((4, 256, QKV), BF16),
            pltpu.VMEM((2, 2, PIECE, QKV), BF16),
            pltpu.VMEM((2, 2, 2, PIECE, QKV), BF16),
            pltpu.VMEM((2, PIECE, QKV), BF16),
            pltpu.VMEM((2, 2, PIECE, QKV), BF16),
            pltpu.VMEM((OWN, QKV), F32),
            pltpu.VMEM((TOK, QKV), BF16),
            pltpu.VMEM((2, TOK, D), BF16),
            pltpu.VMEM((TOK, D // 2), BF16),
            pltpu.VMEM((TOK, QKV), BF16),
            pltpu.VMEM((TOK, QKV), BF16),
            pltpu.VMEM((2, TOK, D), BF16),
            pltpu.VMEM((TOK, D), BF16),
            pltpu.VMEM((TOK, D), BF16),
            pltpu.VMEM((1, D), F32),
            pltpu.VMEM((1, D), F32),
            pltpu.VMEM((8, 1, D), F32),
            dma((4,)),
            dma((32,)),
            dma((32,)),
            dma((2,)),
            dma((2, 2)),
            dma((2,)),
            dma((2,)),
            dma((2, 2)),
            dma((2, 4)),
            dma((4,)),
            dma((8,)),
            dma((2,)),
            dma((2, 2)),
            dma((4,)),
            dma(()),
            dma((8,)),
            dma((SENDS,)),
            dma((16,)),
        ],
        compiler_params=pltpu.CompilerParams(collective_id=0, has_side_effects=True, vmem_limit_bytes=62 << 20),
    )(layer_input[0], resid_grad[0], qkv_grad[0], prev_input[0], prev_qkv_grad[0], qkv_weight[0], norm_gain)
    upstream_grad, weight_grad, gain_grad = pl.pallas_call(
        place,
        out_shape=(
            jax.ShapeDtypeStruct((TOK, D), BF16),
            jax.ShapeDtypeStruct((OWN, QKV), F32),
            jax.ShapeDtypeStruct((1, D), F32),
        ),
        in_specs=[hbm] * 3,
        out_specs=(hbm, hbm, hbm),
        scratch_shapes=[pltpu.VMEM((TOK, D), BF16), pltpu.VMEM((OWN, QKV), F32), pltpu.VMEM((1, D), F32), dma((9,)), dma((9,))],
    )(received, weight_grad, gain_grad)
    return (upstream_grad[None], weight_grad[None], gain_grad)


def solution(mesh):
    tokens, whole = P("section", "fsdp", None), P("section", None)
    return jax.shard_map(
        local,
        mesh=mesh,
        in_specs=(tokens,) * 6 + (whole,),
        out_specs=(tokens, tokens, whole),
        check_vma=False,
    )
```
